32 devices in a mesh: gx: 2 (over x), gy: 16 (over z, y, core).
Axes of the slice: x: 2, y: 2, z: 4, core: 2. Of those that a mesh axis runs over, the one named last changes fastest.
Arguments:
- residual_in: float32 [2, 16, 1024, 256], P('gx', 'gy'), may hold values from -6 to 6
- neumann: float32 [2, 16, 1024, 1024], P('gx', 'gy'), may hold values from -0.1875 to 0.1875
- dirichlet: float32 [2, 16, 1024, 1024], P('gx', 'gy'), may hold values from -0.1875 to 0.1875
- coarse: float32 [2, 1024, 1024], P('gx', 'gy'), may hold values from -0.1875 to 0.1875
- decay: float32 [2, 16, 64], P('gx', 'gy'), may hold values from 0.4 to 1
- face_rows: int32 [2, 16, 1024], P('gx', 'gy'), may hold values from 0 to 1023, each once within a row
- primal: int32 [2, 16, 64], P('gx', 'gy'), may hold values from 0 to 1023, as said below
Outputs:
- solution: float32 [2, 16, 1024, 256], P('gx', 'gy')
- residual: float32 [2, 16, 1024, 256], P('gx', 'gy')
The draws below stay inside these ranges and needn't reach their ends.
Inputs may be any that keep to these rules, and one draw needn't show every extreme that they name: `primal`: each subdomain's 64 entries are distinct rows of its interface. `face_rows`: each subdomain's entries name every interface row once.
All inputs are finite; a program needn't handle non-finite values.
Results may differ from the reference program's by a relative error of at most 0.0001.
Values sent between devices are 32-bit elements; how exact they have to be, the bound alone decides.
A program may use at most 64 MiB of HBM per device.

```python
import jax
import jax.numpy as jnp
from jax import lax

M = 1024
P_SIZE = 64
R = 256
STEPS = 2
SUBX = 2
SUBY = 16
FACE = 256
COARSE = 1024


def draw_primal(key, part):
    keys = jax.random.split(jax.random.fold_in(key, 17), SUBX * SUBY)
    perms = jax.vmap(lambda single: jax.random.permutation(single, M))(keys)
    picked = perms[:, :P_SIZE]
    top_shift = M - 1 - picked[0, 0]
    bottom_shift = (M - picked[1, 0]) % M
    which = jnp.arange(SUBX * SUBY, dtype=jnp.int32)
    offsets = jnp.where(which == 0, top_shift, jnp.where(which == 1, bottom_shift, 0))
    picked = (picked + offsets[:, None]) % M
    return picked.reshape(SUBX, SUBY, P_SIZE).astype(jnp.int32)


def level_of(stream_key, extent, cuts, least, largest):
    level, own = 1.0, jax.random.fold_in(stream_key, 6)
    for axis_at, shards_of in cuts:
        heights = jnp.exp(jax.random.uniform(jax.random.fold_in(own, axis_at), (shards_of,), jnp.float32, least / len(cuts), largest / len(cuts)))
        level = level * jnp.repeat(heights, extent[axis_at] // shards_of).reshape([-1 if axis == axis_at else 1 for axis in range(len(extent))])
    return level


def normal_values(stream_key, shape, width, reach, cuts=(), kind=jnp.bfloat16):
    values = width * jax.random.normal(stream_key, shape, jnp.float32)
    if cuts:
        values = values * level_of(stream_key, shape, cuts, -0.22, 0.18)
    return jnp.clip(values, -reach, reach).astype(kind)


def setup_inputs(seed: int = 0) -> dict:
    key_of = jax.random.split(jax.random.key(seed), 8)
    return {
        "residual_in": normal_values(key_of[0], (SUBX, SUBY, M, R), 1.0, 6.0, ((0, 2), (1, 16)), jnp.float32),
        "neumann": normal_values(key_of[1], (SUBX, SUBY, M, M), M ** -0.5, 0.1875, ((0, 2), (1, 16)), jnp.float32),
        "dirichlet": normal_values(key_of[2], (SUBX, SUBY, M, M), M ** -0.5, 0.1875, ((0, 2), (1, 16)), jnp.float32),
        "coarse": normal_values(key_of[3], (SUBX, COARSE, COARSE), COARSE ** -0.5, 0.1875, ((0, 2), (1, 16)), jnp.float32),
        "decay": jnp.clip(0.4 + 0.6 * jax.random.uniform(key_of[4], (SUBX, SUBY, P_SIZE), jnp.float32) ** level_of(key_of[4], (SUBX, SUBY, P_SIZE), ((0, 2), (1, 16)), -0.2, 0.2), 0.4, 1.0),
        "face_rows": jax.vmap(lambda own: jax.random.permutation(own, M))(jax.random.split(key_of[5], SUBX * SUBY)).reshape((SUBX, SUBY, M)).astype(jnp.int32),
        "primal": draw_primal(jax.random.fold_in(key_of[7], 71), 0),
    }


def neighbours(field, face_rows, inverse):
    faces = jnp.take_along_axis(field, face_rows[..., None], axis=2)
    low_row = faces[:, :, 0:FACE]
    high_row = faces[:, :, FACE:2 * FACE]
    low_col = faces[:, :, 2 * FACE:3 * FACE]
    high_col = faces[:, :, 3 * FACE:4 * FACE]
    zero_row = jnp.zeros_like(low_row[:1])
    zero_col = jnp.zeros_like(low_row[:, :1])
    recv_zero = jnp.concatenate([zero_row, high_row[:-1]], axis=0)
    recv_one = jnp.concatenate([low_row[1:], zero_row], axis=0)
    recv_two = jnp.concatenate([zero_col, high_col[:, :-1]], axis=1)
    recv_three = jnp.concatenate([low_col[:, 1:], zero_col], axis=1)
    stacked = jnp.concatenate([recv_zero, recv_one, recv_two, recv_three], axis=2)
    return jnp.take_along_axis(stacked, inverse[..., None], axis=2)


def reference(residual_in, neumann, dirichlet, coarse, decay, face_rows, primal):
    high = lax.Precision.HIGHEST
    inverse = jnp.argsort(face_rows, axis=-1).astype(jnp.int32)
    onehot = (jnp.arange(M, dtype=jnp.int32)[None, None, :, None] == primal[:, :, None, :]).astype(jnp.float32)
    residual = residual_in
    solution = jnp.zeros_like(residual_in)
    for step in range(STEPS):
        jump = residual - neighbours(residual, face_rows, inverse)
        work = jnp.einsum("xymn,xynr->xymr", neumann, jump, precision=high)
        prim_val = jnp.take_along_axis(work, primal[..., None], axis=2)
        cvec = prim_val.reshape(SUBX, COARSE, R)
        cq = jnp.einsum("xab,xbr->xar", coarse, cvec, precision=high).reshape(SUBX, SUBY, P_SIZE, R)

        def link(prev, item):
            rate, value = item
            current = value + rate[:, :, None] * prev
            return current, current

        start_val = jnp.zeros((SUBY, P_SIZE, R), jnp.float32)
        unused, chain = lax.scan(link, start_val, (decay, cq))
        corrected = work + jnp.einsum("xymp,xypr->xymr", onehot, chain, precision=high)
        update = jnp.einsum("xymn,xynr->xymr", dirichlet, corrected, precision=high)
        solution = solution + update
        residual = jump - 0.5 * update
    return solution, residual
```

```python
import functools

import jax
import jax.numpy as jnp
from jax import lax
from jax.experimental import pallas as pl
from jax.experimental.pallas import tpu as pltpu
from jax.sharding import PartitionSpec as P

STEPS = 2
CUTS = (2, 3)
MESH = pl.DeviceIdType.MESH
F32 = jnp.float32
BF16 = jnp.bfloat16


def dot(a, b):
    return jnp.dot(a, b, preferred_element_type=F32)


def split(x):
    high = x.astype(BF16)
    return high, (x - high.astype(F32)).astype(BF16)


def dot3(a, b):
    return dot(a[0], b[0]) + dot(a[0], b[1]) + dot(a[1], b[0])


def stacked3(a, b):
    rows = a.shape[0] // 2
    first = dot(a, b[0])
    return first[:rows] + first[rows:] + dot(a[:rows], b[1])


def tall3(x):
    high, low = split(x)
    return jnp.concatenate([high, low, high], axis=0)


def when(cond, body):
    if cond is True:
        body()
    else:
        pl.when(cond)(body)


def line_sizes(count):
    chips = count // 2
    inner = 1
    while inner * inner * 4 <= chips:
        inner *= 2
    return chips // inner, inner


def x_slots(nx):
    return 1 if nx == 2 else 2


def kernel(
    nx, ny_all, r_hbm, n_hbm, d_hbm, c_hbm, decay_hbm, rows_hbm, prim_hbm,
    t1_ref, t2_ref, thin_ref, last_ref,
    n_buf, d_buf, nh, nl, dh, dl, perm, perm_t,
    r_buf, jump, upd, fsend, frecv, fix, c_all, cs, psend, gath, qsend, cown, cprev, csend,
    sel, npp, base, decay_v, rows_v, prim_v, esend, erecv, edges, chain_v, hsend, hrecv,
    load_sem, small_sem, cf_ssem, cp_ssem, c_rsem, f_ssem, f_rsem, a_ssem, g_rsem,
    q_ssem, q_rsem, p_ssem, p_rsem, e_ssem, e_rsem, h_ssem, h_rsem, line_sem,
):
    unknowns, width = r_buf.shape
    face = unknowns // 4
    prims = c_all.shape[1]
    nz, ny = line_sizes(ny_all)
    ng = 2 * ny
    part = width // ng
    fold = max(1, 128 // part)
    short = prims // fold
    block = 2 * face
    blocks = unknowns // block
    xs = x_slots(nx)
    slots = xs + 2

    a = lax.axis_index("gx")
    me = lax.axis_index("gy")
    plane = 2 * ny
    core = me % 2
    y = me // 2 % ny
    z = me // plane
    partner = me + 1 - 2 * core

    team = z // ny * ny + y
    g = z % ny * 2 + core

    def member(which, j):
        return ((which // ny * ny + j // 2) * ny + which % ny) * 2 + j % 2

    smalls = [
        pltpu.make_async_copy(src, dst, small_sem.at[i])
        for i, (src, dst) in enumerate(
            [(rows_hbm, rows_v), (prim_hbm, prim_v), (decay_hbm, decay_v)]
        )
    ]
    loads = [
        pltpu.make_async_copy(src, dst, load_sem.at[i])
        for i, (src, dst) in enumerate(
            [(r_hbm, r_buf), (c_hbm, c_all.at[g]), (n_hbm, n_buf), (d_hbm, d_buf)]
        )
    ]
    smalls[0].start()
    loads[0].start()
    smalls[1].start()
    smalls[2].start()

    barrier = pltpu.get_barrier_semaphore()

    def greet(gx, gy):
        pl.semaphore_signal(barrier, inc=1, device_id=(gx, gy), device_id_type=MESH)

    out_slot = xs + core
    in_slot = xs + 1 - core
    outward = me - 1 + 2 * core
    has_out = jnp.logical_and(outward >= 0, outward < ny_all)
    links = [(has_out, (a, outward), out_slot, in_slot)]
    if nx == 2:
        links.append((True, (1 - a, me), 0, 0))
    else:
        links.append((a > 0, (a - 1, me), 0, 1))
        links.append((a < nx - 1, (a + 1, me), 1, 0))
    links.append((True, (a, partner), in_slot, out_slot))
    mate_at = [(g + d) % ng for d in range(ng)]
    mates = [member(team, j) for j in mate_at]
    below, above = z > 0, z < nz - 1
    count = jnp.int32(ng - 1 + plane - 1)
    for has, where, _, _ in links[:-1]:
        when(has, functools.partial(greet, *where))
        count = count + (1 if has is True else has.astype(jnp.int32))
    for d in range(1, ng):
        greet(a, mates[d])
    for d in range(1, plane):
        greet(a, z * plane + (me + d) % plane)
    pl.when(below)(functools.partial(greet, a, me - plane))
    pl.when(above)(functools.partial(greet, a, me + plane))
    count = count + below.astype(jnp.int32) + above.astype(jnp.int32)
    if nx > 1:

        @pl.when(a < 2)
        def _():
            for d in range(1, ng):
                greet(1 - a, mates[d])

        count = count + (a < 2).astype(jnp.int32) * (ng - 1)

    def line_round(turn):
        def tell(low):
            pl.semaphore_signal(
                line_sem.at[turn, 1 if low else 0],
                inc=1,
                device_id=(a, me - plane if low else me + plane),
                device_id_type=MESH,
            )

        pl.when(below)(functools.partial(tell, True))
        pl.when(above)(functools.partial(tell, False))

    def line_wait(turn):
        pl.when(below)(lambda: pl.semaphore_wait(line_sem.at[turn, 0], 1))
        pl.when(above)(lambda: pl.semaphore_wait(line_sem.at[turn, 1], 1))

    turns = [0]

    def advance():
        turn = turns[0]
        if turn < nz - 1:
            line_wait(turn)
            if turn + 1 < nz - 1:
                line_round(turn + 1)
            turns[0] = turn + 1

    def pack(x, pieces=fold):
        size = x.shape[0] // pieces
        return jnp.concatenate([x[j * size : (j + 1) * size] for j in range(pieces)], axis=1)

    def unpack(x, columns=part):
        return jnp.concatenate(
            [x[:, j * columns : (j + 1) * columns] for j in range(x.shape[1] // columns)], axis=0
        )

    def rows_of(i, size):
        if isinstance(i, int):
            return pl.ds(i * size, size)
        return pl.ds(pl.multiple_of(i * size, size), size)

    def remote(src, dst, send, recv, gx, gy):
        return pltpu.make_async_remote_copy(
            src_ref=src, dst_ref=dst, send_sem=send, recv_sem=recv,
            device_id=(gx, gy), device_id_type=MESH,
        )

    def face_copy(step, link):
        _, where, here, there = link
        return remote(
            fsend.at[step, rows_of(here, face), :],
            frecv.at[step, rows_of(there, face), :],
            f_ssem.at[step, here],
            f_rsem.at[step, there],
            *where,
        )

    def face_part(step, link, first, stop):
        _, where, here, there = link
        size = face // 4

        def part_of(slot):
            start = slot * face + first * size
            if not isinstance(slot, int):
                start = pl.multiple_of(start, size)
            return pl.ds(start, (stop - first) * size)

        return remote(
            fsend.at[step, part_of(here), :],
            frecv.at[step, part_of(there), :],
            f_ssem.at[step, here],
            f_rsem.at[step, there],
            *where,
        )

    def send_part(step, first, stop):
        for link in links[:-1]:
            when(link[0], face_part(step, link, first, stop).start)

    def edge_copy(link):
        _, where, here, there = link
        return remote(
            esend.at[here], erecv.at[there], e_ssem.at[here], e_rsem.at[there], *where
        )

    def chain_copy(step, link):
        _, where, here, there = link
        return remote(
            hsend.at[step], hrecv.at[step, there], h_ssem.at[step, here], h_rsem.at[step, there],
            *where,
        )

    def arrives(copy, link):
        has, where, here, _ = link
        when(has, copy((has, where, here, here)).wait_recv)

    lanes = 128

    def face_lines(slot):
        if nx == 2:
            number = 1 - a if isinstance(slot, int) and slot == 0 else slot + 1
        else:
            number = slot
        return rows_v[:, rows_of(number, face)].astype(F32)

    def build_face(slot):
        column = jnp.transpose(jnp.broadcast_to(face_lines(slot), (lanes, face)))
        for t in range(unknowns // lanes):
            cols = lax.broadcasted_iota(jnp.int32, (face, lanes), 1) + t * lanes
            perm[rows_of(slot, face), t * lanes : (t + 1) * lanes] = jnp.where(
                column == cols.astype(F32), 1.0, 0.0
            ).astype(BF16)

    def take_faces(step, field):
        fsend[step] = dot(perm[...], field[0]) + dot(perm[...], field[1])

    smalls[0].wait()
    for slot in range(slots):
        build_face(slot)
    loads[0].wait()
    for load in loads[1:]:
        load.start()
    field = split(r_buf[...])
    take_faces(0, field)
    pl.semaphore_wait(barrier, count)
    for link in links:
        when(link[0], face_copy(0, link).start)
    if nz > 1:
        line_round(0)

    along = [(z + dy) % ny for dy in range(ny)]

    def coarse_far(dy):
        return remote(
            c_all.at[g], c_all.at[g], cf_ssem.at[dy], c_rsem.at[g],
            a, member(team, along[dy] * 2 + core),
        )

    def coarse_near(dy):
        which = along[dy] * 2 + core
        return remote(
            c_all.at[which], c_all.at[which], cp_ssem.at[dy], c_rsem.at[which], a, partner
        )

    def coarse_arrived(which):
        remote(
            c_all.at[which], c_all.at[which], cp_ssem.at[0], c_rsem.at[which], a, partner
        ).wait_recv()

    loads[1].wait()
    coarse_near(0).start()
    for dy in range(1, ny):
        coarse_far(dy).start()

    for link in links[:-1]:
        if link[0] is not True:

            @pl.when(jnp.logical_not(link[0]))
            def _(link=link):
                here = link[2]
                for step in range(STEPS):
                    frecv[step, rows_of(here, face), :] = jnp.zeros((face, width), F32)
                erecv[here] = jnp.zeros(erecv.shape[1:], F32)
                for step in range(STEPS - 1):
                    hrecv[step, here] = jnp.zeros((prims, width), F32)

    lines = jnp.concatenate([face_lines(slot) for slot in range(slots)], axis=1)

    def build_t(i, carry):
        at = rows_of(i, block)
        here = lax.broadcasted_iota(jnp.int32, (block, slots * face), 0) + i * block
        perm_t[at, :] = jnp.where(here.astype(F32) == lines, 1.0, 0.0).astype(BF16)
        return carry

    lax.fori_loop(0, blocks, build_t, 0)

    smalls[1].wait()
    smalls[2].wait()
    eye = lax.broadcasted_iota(jnp.int32, (prims, prims), 0) == lax.broadcasted_iota(
        jnp.int32, (prims, prims), 1
    )
    prim_row = prim_v[...].astype(F32)
    prim_col = jnp.sum(jnp.where(eye, prim_row, 0.0), axis=1, keepdims=True)
    rate = jnp.sum(jnp.where(eye, decay_v[...], 0.0), axis=1, keepdims=True)
    pick_t = jnp.where(
        prim_col == lax.broadcasted_iota(jnp.int32, (prims, unknowns), 1).astype(F32), 1.0, 0.0
    ).astype(BF16)
    thrice = jnp.concatenate([prim_row] * 3, axis=1)
    tops = lax.broadcasted_iota(jnp.int32, (unknowns, 3 * prims), 0).astype(F32) == thrice
    high_side = lax.broadcasted_iota(jnp.int32, (unknowns, 3 * prims), 1) < 2 * prims
    pick_h = jnp.where(jnp.logical_and(tops, high_side), 1.0, 0.0).astype(BF16)
    pick_l = jnp.where(
        jnp.logical_and(tops, jnp.logical_not(high_side)), 1.0, 0.0
    ).astype(BF16)

    loads[2].wait()

    def halve(i, carry):
        at = rows_of(i, block)
        nh[at, :], nl[at, :] = split(n_buf[at, :])
        return carry

    lax.fori_loop(0, blocks, halve, 0)
    advance()
    sel[0:prims, :] = dot(pick_t, nh[...]).astype(BF16)
    sel[prims : 2 * prims, :] = dot(pick_t, nl[...]).astype(BF16)
    advance()
    npp[...] = dot(sel[...], perm_t[...]).astype(BF16)
    base[...] = stacked3(sel[...], field)
    advance()
    loads[3].wait()

    def halve_pick(i, carry):
        at = rows_of(i, block)
        high, low = split(d_buf[at, :])
        dh[at, :] = high
        dl[at, :] = low
        thin_ref[at, :] = (dot(high, pick_h) + dot(low, pick_l)).astype(BF16)
        return carry

    lax.fori_loop(0, blocks, halve_pick, 0)
    for _ in range(nz):
        advance()
    lifted = dot(perm[...], thin_ref[...])
    lifted = lifted[:, :prims] + lifted[:, 2 * prims :]
    for slot in range(slots):
        esend[slot] = pack(lifted[slot * face : (slot + 1) * face], 128 // prims)
    for link in links:
        when(link[0], edge_copy(link).start)

    order = [
        (dz, d)
        for dz in sorted(range(nz), key=lambda dz: -min(dz, nz - dz))
        for d in range(ng)
        if (dz, d) != (0, 0)
    ]

    def spread(step, dz, d):
        return remote(
            psend.at[step, mate_at[d]],
            gath.at[step, me],
            a_ssem.at[step, dz, d],
            g_rsem.at[step, me],
            a,
            member((team + dz) % nz, mate_at[d]),
        )

    def arrived(step, who):
        remote(
            psend.at[step, 0], gath.at[step, who], a_ssem.at[step, 0, 0], g_rsem.at[step, who],
            a, partner,
        ).wait_recv()

    def q_copy(step, d):
        return remote(
            qsend.at[step, mate_at[d]], cown.at[step, g], q_ssem.at[step, d], q_rsem.at[step, g],
            a, mates[d],
        )

    def first_copy(step, d):
        return remote(
            qsend.at[step, mate_at[d]], cprev.at[step, g], p_ssem.at[step, d], p_rsem.at[step, g],
            a + 1, mates[d],
        )

    def next_copy(step, q):
        return remote(
            csend.at[step, q], cprev.at[step, q], p_ssem.at[step, q], p_rsem.at[step, q],
            a + 1, me,
        )

    starts = jnp.logical_and(a == 0, a < nx - 1)
    passes = jnp.logical_and(a > 0, a < nx - 1)

    for step in range(STEPS):
        last = step + 1 == STEPS
        source = r_buf if step == 0 else t2_ref
        for link in links:
            arrives(functools.partial(face_copy, step), link)
        if step == 0:
            ghost = split(frecv[step])
        else:
            ghost = split(frecv[step] - fix[...])
        prim = base[...] - stacked3(npp[...], ghost)
        for q in range(ng):
            psend[step, q] = pack(prim[:, q * part : (q + 1) * part])
        for dz, d in order:
            spread(step, dz, d).start()
        gath[step, me] = psend[step, g]

        def fill(i, carry, source=source, ghost=ghost):
            at = rows_of(i, block)
            back = perm_t[at, :]
            jump[at, :] = source[at, :] - dot(back, ghost[0]) - dot(back, ghost[1])
            return carry

        lax.fori_loop(0, blocks, fill, 0)
        jumps = split(jump[...])

        def multiply(i, carry, jumps=jumps):
            at = rows_of(i, block)
            upd[at, :] = dot3((nh[at, :], nl[at, :]), jumps)
            return carry

        lax.fori_loop(0, blocks, multiply, 0)
        if step == 0:
            for dy in range(1, ny):
                coarse_arrived(along[dy] * 2 + core)
                coarse_near(dy).start()
        works = split(upd[...])

        def smooth(i, carry, works=works, step=step):
            at = rows_of(i, block)
            update = dot3((dh[at, :], dl[at, :]), works)
            if step == 0:
                t1_ref[at, :] = update
            else:
                t1_ref[at, :] += update
            t2_ref[at, :] = jump[at, :] - 0.5 * update
            return carry

        lax.fori_loop(0, blocks, smooth, 0)
        if not last:
            take_faces(step + 1, split(t2_ref[...]))
            send_part(step + 1, 0, CUTS[0])
            face_copy(step + 1, links[-1]).start()
        if step == 0:
            for dy in range(ny):
                coarse_arrived(along[dy] * 2 + 1 - core)
            size = ng * prims
            cs[0:size, :], cs[size : 2 * size, :] = split(
                c_all[...].reshape(size, c_all.shape[2])
            )
        for dz, d in order:
            arrived(step, member((team + dz) % nz, mate_at[d]))
        values = jnp.concatenate([unpack(gath[step, b]) for b in range(ny_all)], axis=0)
        quarter = stacked3(cs[...], split(values))
        for q in range(ng):
            qsend[step, q] = pack(quarter[q * prims : (q + 1) * prims, :])

        @pl.when(starts)
        def _(step=step):
            for d in range(ng):
                first_copy(step, d).start()

        for d in range(1, ng):
            q_copy(step, d).start()
        if not last:
            send_part(step + 1, CUTS[0], CUTS[1])
        cown[step, g] = qsend[step, g]
        if step == 0:
            for link in links:
                arrives(edge_copy, link)
            for slot in range(slots):
                high, low = split(unpack(erecv[slot], prims))
                edges[slot * face : (slot + 1) * face, :] = jnp.concatenate(
                    [high, high, low], axis=1
                )
        for d in range(1, ng):
            remote(
                qsend.at[step, 0], cown.at[step, mate_at[d]], q_ssem.at[step, 0],
                q_rsem.at[step, mate_at[d]], a, partner,
            ).wait_recv()

        def joined(ref, step=step):
            return jnp.concatenate([unpack(ref[step, q]) for q in range(ng)], axis=1)

        @pl.when(a == 0)
        def _(step=step):
            chain_v[...] = joined(cown)

        @pl.when(a > 0)
        def _(step=step):
            for q in range(ng):
                next_copy(step, q).wait_recv()
            chain_v[...] = joined(cown) + rate * joined(cprev)

        @pl.when(passes)
        def _(step=step):
            for q in range(ng):
                csend[step, q] = pack(chain_v[:, q * part : (q + 1) * part])
                next_copy(step, q).start()

        if last:
            last_ref[...] = chain_v[...]
        else:
            hsend[step] = chain_v[...]
            for link in links:
                when(link[0], chain_copy(step, link).start)
            send_part(step + 1, CUTS[1], 4)
            chain = tall3(chain_v[...])

            def finish(i, carry, chain=chain):
                at = rows_of(i, block)
                more = dot(thin_ref[at, :], chain)
                t1_ref[at, :] += more
                t2_ref[at, :] -= 0.5 * more
                return carry

            lax.fori_loop(0, blocks, finish, 0)
            base[...] = stacked3(sel[...], split(t2_ref[...]))
            for link in links:
                arrives(functools.partial(chain_copy, step), link)
            for slot in range(slots):
                at = slice(slot * face, (slot + 1) * face)
                fix[at, :] = 0.5 * dot(edges[at, :], tall3(hrecv[step, slot]))

    coarse_near(0).wait_send()
    for dy in range(1, ny):
        coarse_far(dy).wait_send()
        coarse_near(dy).wait_send()
    for link in links:
        when(link[0], edge_copy(link).wait_send)
    for step in range(STEPS):
        for link in links:
            when(link[0], face_copy(step, link).wait_send)
            if step + 1 < STEPS:
                when(link[0], chain_copy(step, link).wait_send)
        for dz, d in order:
            spread(step, dz, d).wait_send()
        for d in range(1, ng):
            q_copy(step, d).wait_send()

        @pl.when(starts)
        def _(step=step):
            for d in range(ng):
                first_copy(step, d).wait_send()

        @pl.when(passes)
        def _(step=step):
            for q in range(ng):
                next_copy(step, q).wait_send()


def closing(t1, t2, thin, chain, sol, res):
    rows = sol.shape[0]
    at = pl.ds(pl.multiple_of(pl.program_id(0) * rows, rows), rows)
    more = dot(thin[at, :], tall3(chain[...]))
    sol[...] = t1[at, :] + more
    res[...] = t2[at, :] - 0.5 * more


def local(nx, ny_all, residual_in, neumann, dirichlet, coarse, decay, face_rows, primal):
    unknowns, width = residual_in.shape[2:]
    prims = primal.shape[2]
    order = coarse.shape[2]
    nz, ny = line_sizes(ny_all)
    ng = 2 * ny
    part = width // ng
    fold = max(1, 128 // part)
    piece = (prims // fold, fold * part)
    face = unknowns // 4
    slots = x_slots(nx) + 2
    anywhere = pl.BlockSpec(memory_space=pl.ANY)
    inside = pl.BlockSpec(memory_space=pltpu.VMEM)
    square = (unknowns, unknowns)
    field = (unknowns, width)
    ghosts = (slots * face, width)
    edge = (slots, face * prims // 128, 128)
    dma = pltpu.SemaphoreType.DMA
    whole = jax.ShapeDtypeStruct(field, F32)
    outs = [(field, F32), (field, F32), ((unknowns, 3 * prims), BF16), ((prims, width), F32)]
    pieces = pl.pallas_call(
        functools.partial(kernel, nx, ny_all),
        out_shape=tuple(pltpu.VMEM(shape, kind) for shape, kind in outs),
        in_specs=[anywhere] * 7,
        out_specs=(inside,) * 4,
        scratch_shapes=[
            pltpu.VMEM(square, F32),
            pltpu.VMEM(square, F32),
        ]
        + [pltpu.VMEM(square, BF16)] * 4
        + [
            pltpu.VMEM((slots * face, unknowns), BF16),
            pltpu.VMEM((unknowns, slots * face), BF16),
        ]
        + [pltpu.VMEM(field, F32)] * 3
        + [
            pltpu.VMEM((STEPS,) + ghosts, F32),
            pltpu.VMEM((STEPS,) + ghosts, F32),
            pltpu.VMEM(ghosts, F32),
            pltpu.VMEM((ng, prims, order), F32),
            pltpu.VMEM((2 * ng * prims, order), BF16),
            pltpu.VMEM((STEPS, ng) + piece, F32),
            pltpu.VMEM((STEPS, ny_all) + piece, F32),
            pltpu.VMEM((STEPS, ng) + piece, F32),
            pltpu.VMEM((STEPS, ng) + piece, F32),
            pltpu.VMEM((STEPS, ng) + piece, F32),
            pltpu.VMEM((STEPS, ng) + piece, F32),
            pltpu.VMEM((2 * prims, unknowns), BF16),
            pltpu.VMEM((2 * prims, slots * face), BF16),
            pltpu.VMEM((prims, width), F32),
            pltpu.VMEM((1, prims), F32),
            pltpu.VMEM((1, unknowns), jnp.int32),
            pltpu.VMEM((1, prims), jnp.int32),
            pltpu.VMEM(edge, F32),
            pltpu.VMEM(edge, F32),
            pltpu.VMEM((slots * face, 3 * prims), BF16),
            pltpu.VMEM((prims, width), F32),
            pltpu.VMEM((STEPS - 1, prims, width), F32),
            pltpu.VMEM((STEPS - 1, slots, prims, width), F32),
            dma((4,)),
            dma((3,)),
            dma((ny,)),
            dma((ny,)),
            dma((ng,)),
            dma((STEPS, slots)),
            dma((STEPS, slots)),
            dma((STEPS, nz, ng)),
            dma((STEPS, ny_all)),
            dma((STEPS, ng)),
            dma((STEPS, ng)),
            dma((STEPS, ng)),
            dma((STEPS, ng)),
            dma((slots,)),
            dma((slots,)),
            dma((STEPS - 1, slots)),
            dma((STEPS - 1, slots)),
            pltpu.SemaphoreType.REGULAR((max(1, nz - 1), 2)),
        ],
        compiler_params=pltpu.CompilerParams(
            collective_id=0, has_side_effects=True, vmem_limit_bytes=62720 * 1024
        ),
    )(
        residual_in[0, 0],
        neumann[0, 0],
        dirichlet[0, 0],
        coarse[0],
        decay[0],
        face_rows[0],
        primal[0],
    )
    rows = unknowns // 4
    tall = pl.BlockSpec((rows, width), lambda i: (i, 0))
    sol, res = pl.pallas_call(
        closing,
        grid=(unknowns // rows,),
        out_shape=(whole, whole),
        in_specs=[inside] * 4,
        out_specs=(tall, tall),
        compiler_params=pltpu.CompilerParams(vmem_limit_bytes=16000 * 1024),
    )(*pieces)
    return (sol[None, None], res[None, None])


def solution(mesh):
    return jax.shard_map(
        functools.partial(local, mesh.shape["gx"], mesh.shape["gy"]),
        mesh=mesh,
        in_specs=(
            P("gx", "gy", None, None),
            P("gx", "gy", None, None),
            P("gx", "gy", None, None),
            P("gx", "gy", None),
            P("gx", "gy", None),
            P("gx", "gy", None),
            P("gx", "gy", None),
        ),
        out_specs=(P("gx", "gy", None, None), P("gx", "gy", None, None)),
        check_vma=False,
    )
```

```python
import functools

import jax
import jax.numpy as jnp
from jax import lax
from jax.experimental import pallas as pl
from jax.experimental.pallas import tpu as pltpu
from jax.sharding import PartitionSpec as P

STEPS = 2
CUTS = (0, 2, 4, 4)
UP_CUTS = (0, 1, 4, 4)
DOWN_CUTS = (0, 4, 4, 4)
MESH = pl.DeviceIdType.MESH
F32 = jnp.float32
BF16 = jnp.bfloat16


def dot(a, b):
    return jnp.dot(a, b, preferred_element_type=F32)


def split(x):
    high = x.astype(BF16)
    return high, (x - high.astype(F32)).astype(BF16)


def dot3(a, b):
    return dot(a[0], b[0]) + dot(a[0], b[1]) + dot(a[1], b[0])


def stacked3(a, b):
    rows = a.shape[0] // 2
    first = dot(a, b[0])
    return first[:rows] + first[rows:] + dot(a[:rows], b[1])


def tall3(x):
    high, low = split(x)
    return jnp.concatenate([high, low, high], axis=0)


def when(cond, body):
    if cond is True:
        body()
    elif cond is not False:
        pl.when(cond)(body)


def both(p, q):
    if p is True or q is False:
        return q
    if q is True or p is False:
        return p
    return jnp.logical_and(p, q)


def negate(p):
    return not p if isinstance(p, bool) else jnp.logical_not(p)


def line_sizes(count):
    chips = count // 2
    inner = 1
    while inner * inner * 4 <= chips:
        inner *= 2
    return chips // inner, inner


def x_slots(nx):
    return 1 if nx == 2 else 2


def kernel(
    nx, ny_all, r_hbm, n_hbm, d_hbm, c_hbm, decay_hbm, rows_hbm, prim_hbm,
    t1_ref, t2_ref, thin_ref, last_ref,
    n_buf, d_buf, nh, nl, dh, dl, perm, perm_t,
    r_buf, jump, high_v, low_v, high_w, low_w, fsend, frecv, fix, c_all, cs, psend, gath, qsend, cown, cprev, csend,
    sel, npp, base, decay_v, rows_v, prim_v, esend, erecv, edges, chain_v, hsend, hrecv,
    load_sem, small_sem, cf_ssem, cp_ssem, c_rsem, f_ssem, f_rsem, a_ssem, g_rsem,
    q_ssem, q_rsem, p_ssem, p_rsem, e_ssem, e_rsem, h_ssem, h_rsem, line_sem,
):
    unknowns, width = r_buf.shape
    face = unknowns // 4
    prims = c_all.shape[1]
    nz, ny = line_sizes(ny_all)
    ng = 2 * ny
    part = width // ng
    fold = max(1, 128 // part)
    short = prims // fold
    block = 2 * face
    blocks = unknowns // block
    xs = x_slots(nx)
    slots = xs + 2

    a = lax.axis_index("gx")
    me = lax.axis_index("gy")
    plane = 2 * ny
    core = me % 2
    y = me // 2 % ny
    z = me // plane
    partner = me + 1 - 2 * core

    team = z // ny * ny + y
    g = z % ny * 2 + core

    def member(which, j):
        return ((which // ny * ny + j // 2) * ny + which % ny) * 2 + j % 2

    smalls = [
        pltpu.make_async_copy(src, dst, small_sem.at[i])
        for i, (src, dst) in enumerate(
            [(rows_hbm, rows_v), (prim_hbm, prim_v), (decay_hbm, decay_v)]
        )
    ]
    loads = [
        pltpu.make_async_copy(src, dst, load_sem.at[i])
        for i, (src, dst) in enumerate(
            [(r_hbm, r_buf), (c_hbm, c_all.at[g]), (n_hbm, n_buf), (d_hbm, d_buf)]
        )
    ]
    smalls[0].start()
    loads[0].start()
    smalls[1].start()
    smalls[2].start()

    barrier = pltpu.get_barrier_semaphore()

    def greet(gx, gy):
        pl.semaphore_signal(barrier, inc=1, device_id=(gx, gy), device_id_type=MESH)

    out_slot = xs + core
    in_slot = xs + 1 - core
    outward = me - 1 + 2 * core
    has_out = jnp.logical_and(outward >= 0, outward < ny_all)
    links = [(has_out, (a, outward), out_slot, in_slot, None)]
    if nx == 2:
        links.append((True, (1 - a, me), 0, 0, a == 0))
    else:
        links.append((a > 0, (a - 1, me), 0, 1, False))
        links.append((a < nx - 1, (a + 1, me), 1, 0, True))
    links.append((True, (a, partner), in_slot, out_slot, None))
    mate_at = [(g + d) % ng for d in range(ng)]
    mates = [member(team, j) for j in mate_at]
    below, above = z > 0, z < nz - 1
    count = jnp.int32(ng - 1 + plane - 1)
    for has, where, _, _, _ in links[:-1]:
        when(has, functools.partial(greet, *where))
        count = count + (1 if has is True else has.astype(jnp.int32))
    for d in range(1, ng):
        greet(a, mates[d])
    for d in range(1, plane):
        greet(a, z * plane + (me + d) % plane)
    pl.when(below)(functools.partial(greet, a, me - plane))
    pl.when(above)(functools.partial(greet, a, me + plane))
    count = count + below.astype(jnp.int32) + above.astype(jnp.int32)
    if nx > 1:

        @pl.when(a < 2)
        def _():
            for d in range(1, ng):
                greet(1 - a, mates[d])

        count = count + (a < 2).astype(jnp.int32) * (ng - 1)

    def line_round(turn):
        def tell(low):
            pl.semaphore_signal(
                line_sem.at[turn, 1 if low else 0],
                inc=1,
                device_id=(a, me - plane if low else me + plane),
                device_id_type=MESH,
            )

        pl.when(below)(functools.partial(tell, True))
        pl.when(above)(functools.partial(tell, False))

    def line_wait(turn):
        pl.when(below)(lambda: pl.semaphore_wait(line_sem.at[turn, 0], 1))
        pl.when(above)(lambda: pl.semaphore_wait(line_sem.at[turn, 1], 1))

    turns = [0]

    def advance():
        turn = turns[0]
        if turn < nz - 1:
            line_wait(turn)
            if turn + 1 < nz - 1:
                line_round(turn + 1)
            turns[0] = turn + 1

    def pack(x, pieces=fold):
        size = x.shape[0] // pieces
        return jnp.concatenate([x[j * size : (j + 1) * size] for j in range(pieces)], axis=1)

    def unpack(x, columns=part):
        return jnp.concatenate(
            [x[:, j * columns : (j + 1) * columns] for j in range(x.shape[1] // columns)], axis=0
        )

    def rows_of(i, size):
        if isinstance(i, int):
            return pl.ds(i * size, size)
        return pl.ds(pl.multiple_of(i * size, size), size)

    def remote(src, dst, send, recv, gx, gy):
        return pltpu.make_async_remote_copy(
            src_ref=src, dst_ref=dst, send_sem=send, recv_sem=recv,
            device_id=(gx, gy), device_id_type=MESH,
        )

    def face_copy(step, link):
        _, where, here, there, _ = link
        return remote(
            fsend.at[step, rows_of(here, face), :],
            frecv.at[step, rows_of(there, face), :],
            f_ssem.at[step, here],
            f_rsem.at[step, there],
            *where,
        )

    def face_part(step, link, first, stop):
        _, where, here, there, _ = link
        size = face // 4

        def part_of(slot):
            start = slot * face + first * size
            if not isinstance(slot, int):
                start = pl.multiple_of(start, size)
            return pl.ds(start, (stop - first) * size)

        return remote(
            fsend.at[step, part_of(here), :],
            frecv.at[step, part_of(there), :],
            f_ssem.at[step, here],
            f_rsem.at[step, there],
            *where,
        )

    def send_part(step, stage, some):
        for link in some:
            for up, cuts in ((None, CUTS), (True, UP_CUTS), (False, DOWN_CUTS)):
                first, stop = cuts[stage], cuts[stage + 1]
                if first == stop or (up is None) != (link[4] is None):
                    continue
                side = True if up is None else link[4] if up else negate(link[4])
                when(both(link[0], side), face_part(step, link, first, stop).start)

    def edge_copy(link):
        _, where, here, there, _ = link
        return remote(
            esend.at[here], erecv.at[there], e_ssem.at[here], e_rsem.at[there], *where
        )

    def chain_copy(step, link):
        _, where, here, there, _ = link
        return remote(
            hsend.at[step], hrecv.at[step, there], h_ssem.at[step, here], h_rsem.at[step, there],
            *where,
        )

    def arrives(copy, link, cond=True):
        has, where, here, _, up = link
        when(both(has, cond), copy((has, where, here, here, up)).wait_recv)

    def comes_down(link):
        return True if link[4] is None else link[4]

    def goes_down(link):
        return True if link[4] is None else negate(link[4])

    lanes = 128

    def face_lines(slot):
        if nx == 2:
            number = 1 - a if isinstance(slot, int) and slot == 0 else slot + 1
        else:
            number = slot
        return rows_v[:, rows_of(number, face)].astype(F32)

    def build_face(slot):
        column = jnp.transpose(jnp.broadcast_to(face_lines(slot), (lanes, face)))
        for t in range(unknowns // lanes):
            cols = lax.broadcasted_iota(jnp.int32, (face, lanes), 1) + t * lanes
            perm[rows_of(slot, face), t * lanes : (t + 1) * lanes] = jnp.where(
                column == cols.astype(F32), 1.0, 0.0
            ).astype(BF16)

    def take_faces(step, field, some):
        for slot in some:
            at = slice(slot * face, (slot + 1) * face)
            picks = perm[at, :]
            fsend[step, at, :] = dot(picks, field[0]) + dot(picks, field[1])

    smalls[0].wait()
    for slot in range(slots):
        build_face(slot)
    loads[0].wait()
    for load in loads[1:]:
        load.start()
    field = split(r_buf[...])
    take_faces(0, field, range(xs, slots))
    pl.semaphore_wait(barrier, count)
    when(links[0][0], face_copy(0, links[0]).start)
    take_faces(0, field, range(xs))
    for link in links[1:]:
        when(link[0], face_copy(0, link).start)
    if nz > 1:
        line_round(0)

    along = [(z + dy) % ny for dy in range(ny)]

    def coarse_far(dy):
        return remote(
            c_all.at[g], c_all.at[g], cf_ssem.at[dy], c_rsem.at[g],
            a, member(team, along[dy] * 2 + core),
        )

    def coarse_near(dy):
        which = along[dy] * 2 + core
        return remote(
            c_all.at[which], c_all.at[which], cp_ssem.at[dy], c_rsem.at[which], a, partner
        )

    def coarse_arrived(which):
        remote(
            c_all.at[which], c_all.at[which], cp_ssem.at[0], c_rsem.at[which], a, partner
        ).wait_recv()

    loads[1].wait()
    coarse_near(0).start()
    for dy in range(1, ny):
        coarse_far(dy).start()

    for link in links[:-1]:
        if link[0] is not True:

            @pl.when(jnp.logical_not(link[0]))
            def _(link=link):
                here = link[2]
                for step in range(STEPS):
                    frecv[step, rows_of(here, face), :] = jnp.zeros((face, width), F32)
                erecv[here] = jnp.zeros(erecv.shape[1:], F32)
                for step in range(STEPS - 1):
                    hrecv[step, here] = jnp.zeros((prims, width), F32)

    lines = jnp.concatenate([face_lines(slot) for slot in range(slots)], axis=1)

    def build_t(i, carry):
        at = rows_of(i, block)
        here = lax.broadcasted_iota(jnp.int32, (block, slots * face), 0) + i * block
        perm_t[at, :] = jnp.where(here.astype(F32) == lines, 1.0, 0.0).astype(BF16)
        return carry

    lax.fori_loop(0, blocks, build_t, 0)

    smalls[1].wait()
    smalls[2].wait()
    eye = lax.broadcasted_iota(jnp.int32, (prims, prims), 0) == lax.broadcasted_iota(
        jnp.int32, (prims, prims), 1
    )
    prim_row = prim_v[...].astype(F32)
    prim_col = jnp.sum(jnp.where(eye, prim_row, 0.0), axis=1, keepdims=True)
    rate = jnp.sum(jnp.where(eye, decay_v[...], 0.0), axis=1, keepdims=True)
    pick_t = jnp.where(
        prim_col == lax.broadcasted_iota(jnp.int32, (prims, unknowns), 1).astype(F32), 1.0, 0.0
    ).astype(BF16)
    thrice = jnp.concatenate([prim_row] * 3, axis=1)
    tops = lax.broadcasted_iota(jnp.int32, (unknowns, 3 * prims), 0).astype(F32) == thrice
    high_side = lax.broadcasted_iota(jnp.int32, (unknowns, 3 * prims), 1) < 2 * prims
    pick_h = jnp.where(jnp.logical_and(tops, high_side), 1.0, 0.0).astype(BF16)
    pick_l = jnp.where(
        jnp.logical_and(tops, jnp.logical_not(high_side)), 1.0, 0.0
    ).astype(BF16)
    loads[2].wait()

    def halve(i, carry):
        at = rows_of(i, block)
        nh[at, :], nl[at, :] = split(n_buf[at, :])
        return carry

    lax.fori_loop(0, blocks, halve, 0)
    advance()
    sel[0:prims, :] = dot(pick_t, nh[...]).astype(BF16)
    sel[prims : 2 * prims, :] = dot(pick_t, nl[...]).astype(BF16)
    advance()
    npp[...] = dot(sel[...], perm_t[...]).astype(BF16)
    base[...] = stacked3(sel[...], field)
    advance()
    loads[3].wait()

    def halve_pick(i, carry):
        at = rows_of(i, block)
        high, low = split(d_buf[at, :])
        dh[at, :] = high
        dl[at, :] = low
        thin_ref[at, :] = (dot(high, pick_h) + dot(low, pick_l)).astype(BF16)
        return carry

    lax.fori_loop(0, blocks, halve_pick, 0)
    for _ in range(nz):
        advance()
    lifted = dot(perm[...], thin_ref[...])
    lifted = lifted[:, :prims] + lifted[:, 2 * prims :]
    for slot in range(slots):
        esend[slot] = pack(lifted[slot * face : (slot + 1) * face], 128 // prims)
    for link in links:
        when(link[0], edge_copy(link).start)

    order = [
        (dz, d)
        for dz in sorted(range(nz), key=lambda dz: -min(dz, nz - dz))
        for d in range(ng)
        if (dz, d) != (0, 0)
    ]

    def spread(step, dz, d):
        return remote(
            psend.at[step, mate_at[d]],
            gath.at[step, me],
            a_ssem.at[step, dz, d],
            g_rsem.at[step, me],
            a,
            member((team + dz) % nz, mate_at[d]),
        )

    def arrived(step, who):
        remote(
            psend.at[step, 0], gath.at[step, who], a_ssem.at[step, 0, 0], g_rsem.at[step, who],
            a, partner,
        ).wait_recv()

    def q_copy(step, d):
        return remote(
            qsend.at[step, mate_at[d]], cown.at[step, g], q_ssem.at[step, d], q_rsem.at[step, g],
            a, mates[d],
        )

    def first_copy(step, d):
        return remote(
            qsend.at[step, mate_at[d]], cprev.at[step, g], p_ssem.at[step, d], p_rsem.at[step, g],
            a + 1, mates[d],
        )

    def next_copy(step, q):
        return remote(
            csend.at[step, q], cprev.at[step, q], p_ssem.at[step, q], p_rsem.at[step, q],
            a + 1, me,
        )

    starts = jnp.logical_and(a == 0, a < nx - 1)
    passes = jnp.logical_and(a > 0, a < nx - 1)

    for step in range(STEPS):
        last = step + 1 == STEPS
        source = r_buf if step == 0 else t2_ref
        for link in links:
            arrives(functools.partial(face_copy, step), link)
        if step == 0:
            ghost = split(frecv[step])
        else:
            ghost = split(frecv[step] - fix[...])
        prim = base[...] - stacked3(npp[...], ghost)
        for q in range(ng):
            psend[step, q] = pack(prim[:, q * part : (q + 1) * part])
        for dz, d in order:
            spread(step, dz, d).start()
        gath[step, me] = psend[step, g]

        def fill(i, carry, source=source, ghost=ghost):
            at = rows_of(i, block)
            back = perm_t[at, :]
            value = source[at, :] - dot(back, ghost[0]) - dot(back, ghost[1])
            jump[at, :] = value
            high_v[at, :], low_v[at, :] = split(value)
            return carry

        lax.fori_loop(0, blocks, fill, 0)

        def multiply(i, carry):
            at = rows_of(i, block)
            work = dot3((nh[at, :], nl[at, :]), (high_v[...], low_v[...]))
            high_w[at, :], low_w[at, :] = split(work)
            return carry

        lax.fori_loop(0, blocks, multiply, 0)
        if step == 0:
            for dy in range(1, ny):
                coarse_arrived(along[dy] * 2 + core)
                coarse_near(dy).start()

        def smooth(i, carry, step=step, last=last):
            at = rows_of(i, block)
            update = dot3((dh[at, :], dl[at, :]), (high_w[...], low_w[...]))
            if step == 0:
                t1_ref[at, :] = update
            else:
                t1_ref[at, :] += update
            rest = jump[at, :] - 0.5 * update
            t2_ref[at, :] = rest
            if not last:
                high_v[at, :], low_v[at, :] = split(rest)
            return carry

        lax.fori_loop(0, blocks, smooth, 0)
        if not last:
            rests = (high_v[...], low_v[...])
            take_faces(step + 1, rests, range(xs, slots))
            send_part(step + 1, 0, links[:1])
            take_faces(step + 1, rests, range(xs))
            send_part(step + 1, 0, links[1:-1])
            face_copy(step + 1, links[-1]).start()
        if step == 0:
            for dy in range(ny):
                coarse_arrived(along[dy] * 2 + 1 - core)
            size = ng * prims
            cs[0:size, :], cs[size : 2 * size, :] = split(
                c_all[...].reshape(size, c_all.shape[2])
            )
        for dz, d in order:
            arrived(step, member((team + dz) % nz, mate_at[d]))
        values = jnp.concatenate([unpack(gath[step, b]) for b in range(ny_all)], axis=0)
        quarter = stacked3(cs[...], split(values))
        for q in range(ng):
            qsend[step, q] = pack(quarter[q * prims : (q + 1) * prims, :])

        @pl.when(starts)
        def _(step=step):
            for d in range(ng):
                first_copy(step, d).start()

        for d in range(1, ng):
            q_copy(step, d).start()
        if not last:
            send_part(step + 1, 1, links[:-1])
        cown[step, g] = qsend[step, g]
        for d in range(1, ng):
            remote(
                qsend.at[step, 0], cown.at[step, mate_at[d]], q_ssem.at[step, 0],
                q_rsem.at[step, mate_at[d]], a, partner,
            ).wait_recv()

        def joined(ref, step=step):
            return jnp.concatenate([unpack(ref[step, q]) for q in range(ng)], axis=1)

        @pl.when(a == 0)
        def _(step=step):
            chain_v[...] = joined(cown)

        @pl.when(a > 0)
        def _(step=step):
            for q in range(ng):
                next_copy(step, q).wait_recv()
            chain_v[...] = joined(cown) + rate * joined(cprev)

        @pl.when(passes)
        def _(step=step):
            for q in range(ng):
                csend[step, q] = pack(chain_v[:, q * part : (q + 1) * part])
                next_copy(step, q).start()

        if last:
            last_ref[...] = chain_v[...]
        else:
            hsend[step] = chain_v[...]
            for link in links:
                when(both(link[0], goes_down(link)), chain_copy(step, link).start)
            send_part(step + 1, 2, links[:-1])
            if nx > 1:

                @pl.when(a > 0)
                def _(step=step):
                    hrecv[step, 0] = joined(cprev)

            chain = tall3(chain_v[...])

            def finish(i, carry, chain=chain):
                at = rows_of(i, block)
                more = dot(thin_ref[at, :], chain)
                t1_ref[at, :] += more
                t2_ref[at, :] -= 0.5 * more
                return carry

            lax.fori_loop(0, blocks, finish, 0)
            base[...] = stacked3(sel[...], split(t2_ref[...]))
            if step == 0:
                for link in links:
                    arrives(edge_copy, link)
                for slot in range(slots):
                    high, low = split(unpack(erecv[slot], prims))
                    edges[slot * face : (slot + 1) * face, :] = jnp.concatenate(
                        [high, high, low], axis=1
                    )
            for link in links:
                arrives(functools.partial(chain_copy, step), link, comes_down(link))
            for slot in range(slots):
                at = slice(slot * face, (slot + 1) * face)
                fix[at, :] = 0.5 * dot(edges[at, :], tall3(hrecv[step, slot]))

    coarse_near(0).wait_send()
    for dy in range(1, ny):
        coarse_far(dy).wait_send()
        coarse_near(dy).wait_send()
    for link in links:
        when(link[0], edge_copy(link).wait_send)
    for step in range(STEPS):
        for link in links:
            when(link[0], face_copy(step, link).wait_send)
            if step + 1 < STEPS:
                when(both(link[0], goes_down(link)), chain_copy(step, link).wait_send)
        for dz, d in order:
            spread(step, dz, d).wait_send()
        for d in range(1, ng):
            q_copy(step, d).wait_send()

        @pl.when(starts)
        def _(step=step):
            for d in range(ng):
                first_copy(step, d).wait_send()

        @pl.when(passes)
        def _(step=step):
            for q in range(ng):
                next_copy(step, q).wait_send()


def closing(t1, t2, thin, chain, sol, res):
    rows = sol.shape[0]
    at = pl.ds(pl.multiple_of(pl.program_id(0) * rows, rows), rows)
    more = dot(thin[at, :], tall3(chain[...]))
    sol[...] = t1[at, :] + more
    res[...] = t2[at, :] - 0.5 * more


def local(nx, ny_all, residual_in, neumann, dirichlet, coarse, decay, face_rows, primal):
    unknowns, width = residual_in.shape[2:]
    prims = primal.shape[2]
    order = coarse.shape[2]
    nz, ny = line_sizes(ny_all)
    ng = 2 * ny
    part = width // ng
    fold = max(1, 128 // part)
    piece = (prims // fold, fold * part)
    face = unknowns // 4
    slots = x_slots(nx) + 2
    anywhere = pl.BlockSpec(memory_space=pl.ANY)
    inside = pl.BlockSpec(memory_space=pltpu.VMEM)
    square = (unknowns, unknowns)
    field = (unknowns, width)
    ghosts = (slots * face, width)
    edge = (slots, face * prims // 128, 128)
    dma = pltpu.SemaphoreType.DMA
    whole = jax.ShapeDtypeStruct(field, F32)
    outs = [(field, F32), (field, F32), ((unknowns, 3 * prims), BF16), ((prims, width), F32)]
    pieces = pl.pallas_call(
        functools.partial(kernel, nx, ny_all),
        out_shape=tuple(pltpu.VMEM(shape, kind) for shape, kind in outs),
        in_specs=[anywhere] * 7,
        out_specs=(inside,) * 4,
        scratch_shapes=[
            pltpu.VMEM(square, F32),
            pltpu.VMEM(square, F32),
        ]
        + [pltpu.VMEM(square, BF16)] * 4
        + [
            pltpu.VMEM((slots * face, unknowns), BF16),
            pltpu.VMEM((unknowns, slots * face), BF16),
        ]
        + [pltpu.VMEM(field, F32)] * 2
        + [pltpu.VMEM(field, BF16)] * 4
        + [
            pltpu.VMEM((STEPS,) + ghosts, F32),
            pltpu.VMEM((STEPS,) + ghosts, F32),
            pltpu.VMEM(ghosts, F32),
            pltpu.VMEM((ng, prims, order), F32),
            pltpu.VMEM((2 * ng * prims, order), BF16),
            pltpu.VMEM((STEPS, ng) + piece, F32),
            pltpu.VMEM((STEPS, ny_all) + piece, F32),
            pltpu.VMEM((STEPS, ng) + piece, F32),
            pltpu.VMEM((STEPS, ng) + piece, F32),
            pltpu.VMEM((STEPS, ng) + piece, F32),
            pltpu.VMEM((STEPS, ng) + piece, F32),
            pltpu.VMEM((2 * prims, unknowns), BF16),
            pltpu.VMEM((2 * prims, slots * face), BF16),
            pltpu.VMEM((prims, width), F32),
            pltpu.VMEM((1, prims), F32),
            pltpu.VMEM((1, unknowns), jnp.int32),
            pltpu.VMEM((1, prims), jnp.int32),
            pltpu.VMEM(edge, F32),
            pltpu.VMEM(edge, F32),
            pltpu.VMEM((slots * face, 3 * prims), BF16),
            pltpu.VMEM((prims, width), F32),
            pltpu.VMEM((STEPS - 1, prims, width), F32),
            pltpu.VMEM((STEPS - 1, slots, prims, width), F32),
            dma((4,)),
            dma((3,)),
            dma((ny,)),
            dma((ny,)),
            dma((ng,)),
            dma((STEPS, slots)),
            dma((STEPS, slots)),
            dma((STEPS, nz, ng)),
            dma((STEPS, ny_all)),
            dma((STEPS, ng)),
            dma((STEPS, ng)),
            dma((STEPS, ng)),
            dma((STEPS, ng)),
            dma((slots,)),
            dma((slots,)),
            dma((STEPS - 1, slots)),
            dma((STEPS - 1, slots)),
            pltpu.SemaphoreType.REGULAR((max(1, nz - 1), 2)),
        ],
        compiler_params=pltpu.CompilerParams(
            collective_id=0, has_side_effects=True, vmem_limit_bytes=62720 * 1024
        ),
    )(
        residual_in[0, 0],
        neumann[0, 0],
        dirichlet[0, 0],
        coarse[0],
        decay[0],
        face_rows[0],
        primal[0],
    )
    rows = unknowns // 4
    tall = pl.BlockSpec((rows, width), lambda i: (i, 0))
    sol, res = pl.pallas_call(
        closing,
        grid=(unknowns // rows,),
        out_shape=(whole, whole),
        in_specs=[inside] * 4,
        out_specs=(tall, tall),
        compiler_params=pltpu.CompilerParams(vmem_limit_bytes=16000 * 1024),
    )(*pieces)
    return (sol[None, None], res[None, None])


def solution(mesh):
    return jax.shard_map(
        functools.partial(local, mesh.shape["gx"], mesh.shape["gy"]),
        mesh=mesh,
        in_specs=(
            P("gx", "gy", None, None),
            P("gx", "gy", None, None),
            P("gx", "gy", None, None),
            P("gx", "gy", None),
            P("gx", "gy", None),
            P("gx", "gy", None),
            P("gx", "gy", None),
        ),
        out_specs=(P("gx", "gy", None, None), P("gx", "gy", None, None)),
        check_vma=False,
    )
```

```python
import functools

import jax
import jax.numpy as jnp
from jax import lax
from jax.experimental import pallas as pl
from jax.experimental.pallas import tpu as pltpu
from jax.sharding import PartitionSpec as P

STEPS = 2
CUTS = (0, 4, 8, 8)
UP_CUTS = (0, 3, 8, 8)
DOWN_CUTS = (0, 8, 8, 8)
MESH = pl.DeviceIdType.MESH
F32 = jnp.float32
BF16 = jnp.bfloat16


def dot(a, b):
    return jnp.dot(a, b, preferred_element_type=F32)


def split(x):
    high = x.astype(BF16)
    return high, (x - high.astype(F32)).astype(BF16)


def dot3(a, b):
    return dot(a[0], b[0]) + dot(a[0], b[1]) + dot(a[1], b[0])


def stacked3(a, b):
    rows = a.shape[0] // 2
    first = dot(a, b[0])
    return first[:rows] + first[rows:] + dot(a[:rows], b[1])


def tall3(x):
    high, low = split(x)
    return jnp.concatenate([high, low, high], axis=0)


def when(cond, body):
    if cond is True:
        body()
    elif cond is not False:
        pl.when(cond)(body)


def both(p, q):
    if p is True or q is False:
        return q
    if q is True or p is False:
        return p
    return jnp.logical_and(p, q)


def negate(p):
    return not p if isinstance(p, bool) else jnp.logical_not(p)


def line_sizes(count):
    chips = count // 2
    inner = 1
    while inner * inner * 4 <= chips:
        inner *= 2
    return chips // inner, inner


def x_slots(nx):
    return 1 if nx == 2 else 2


def kernel(
    nx, ny_all, r_hbm, n_hbm, d_hbm, c_hbm, decay_hbm, rows_hbm, prim_hbm,
    t1_ref, t2_ref, thin_ref, last_ref,
    n_buf, d_buf, nh, nl, dh, dl, perm, perm_t,
    r_buf, jump, high_v, low_v, high_w, low_w, fsend, frecv, fix, c_all, cs, psend, gath, qsend, cown, cprev, csend,
    sel, npp, base, decay_v, rows_v, prim_v, esend, erecv, edges, couple, chain_v, hsend, hrecv,
    load_sem, small_sem, cf_ssem, cp_ssem, c_rsem, f_ssem, f_rsem, a_ssem, g_rsem,
    q_ssem, q_rsem, p_ssem, p_rsem, e_ssem, e_rsem, h_ssem, h_rsem, line_sem,
):
    unknowns, width = r_buf.shape
    face = unknowns // 4
    prims = c_all.shape[1]
    nz, ny = line_sizes(ny_all)
    ng = 2 * ny
    part = width // ng
    fold = max(1, 128 // part)
    short = prims // fold
    block = 2 * face
    blocks = unknowns // block
    xs = x_slots(nx)
    slots = xs + 2

    a = lax.axis_index("gx")
    me = lax.axis_index("gy")
    plane = 2 * ny
    core = me % 2
    y = me // 2 % ny
    z = me // plane
    partner = me + 1 - 2 * core

    team = z // ny * ny + y
    g = z % ny * 2 + core

    def member(which, j):
        return ((which // ny * ny + j // 2) * ny + which % ny) * 2 + j % 2

    smalls = [
        pltpu.make_async_copy(src, dst, small_sem.at[i])
        for i, (src, dst) in enumerate(
            [(rows_hbm, rows_v), (prim_hbm, prim_v), (decay_hbm, decay_v)]
        )
    ]
    loads = [
        pltpu.make_async_copy(src, dst, load_sem.at[i])
        for i, (src, dst) in enumerate(
            [(r_hbm, r_buf), (c_hbm, c_all.at[g]), (n_hbm, n_buf), (d_hbm, d_buf)]
        )
    ]
    smalls[0].start()
    loads[0].start()
    smalls[1].start()
    smalls[2].start()

    barrier = pltpu.get_barrier_semaphore()

    def greet(gx, gy):
        pl.semaphore_signal(barrier, inc=1, device_id=(gx, gy), device_id_type=MESH)

    out_slot = xs + core
    in_slot = xs + 1 - core
    outward = me - 1 + 2 * core
    has_out = jnp.logical_and(outward >= 0, outward < ny_all)
    links = [(has_out, (a, outward), out_slot, in_slot, None)]
    if nx == 2:
        links.append((True, (1 - a, me), 0, 0, a == 0))
    else:
        links.append((a > 0, (a - 1, me), 0, 1, False))
        links.append((a < nx - 1, (a + 1, me), 1, 0, True))
    links.append((True, (a, partner), in_slot, out_slot, None))
    mate_at = [(g + d) % ng for d in range(ng)]
    mates = [member(team, j) for j in mate_at]
    below, above = z > 0, z < nz - 1
    count = jnp.int32(ng - 1 + plane - 1)
    for has, where, _, _, _ in links[:-1]:
        when(has, functools.partial(greet, *where))
        count = count + (1 if has is True else has.astype(jnp.int32))
    for d in range(1, ng):
        greet(a, mates[d])
    for d in range(1, plane):
        greet(a, z * plane + (me + d) % plane)
    pl.when(below)(functools.partial(greet, a, me - plane))
    pl.when(above)(functools.partial(greet, a, me + plane))
    count = count + below.astype(jnp.int32) + above.astype(jnp.int32)
    if nx > 1:

        @pl.when(a < 2)
        def _():
            for d in range(1, ng):
                greet(1 - a, mates[d])

        count = count + (a < 2).astype(jnp.int32) * (ng - 1)

    def line_round(turn):
        def tell(low):
            pl.semaphore_signal(
                line_sem.at[turn, 1 if low else 0],
                inc=1,
                device_id=(a, me - plane if low else me + plane),
                device_id_type=MESH,
            )

        pl.when(below)(functools.partial(tell, True))
        pl.when(above)(functools.partial(tell, False))

    def line_wait(turn):
        pl.when(below)(lambda: pl.semaphore_wait(line_sem.at[turn, 0], 1))
        pl.when(above)(lambda: pl.semaphore_wait(line_sem.at[turn, 1], 1))

    turns = [0]

    def advance():
        turn = turns[0]
        if turn < nz - 1:
            line_wait(turn)
            if turn + 1 < nz - 1:
                line_round(turn + 1)
            turns[0] = turn + 1

    def pack(x, pieces=fold):
        size = x.shape[0] // pieces
        return jnp.concatenate([x[j * size : (j + 1) * size] for j in range(pieces)], axis=1)

    def unpack(x, columns=part):
        return jnp.concatenate(
            [x[:, j * columns : (j + 1) * columns] for j in range(x.shape[1] // columns)], axis=0
        )

    apart = pl.when(a >= 0)

    def rows_of(i, size):
        if isinstance(i, int):
            return pl.ds(i * size, size)
        return pl.ds(pl.multiple_of(i * size, size), size)

    def remote(src, dst, send, recv, gx, gy):
        return pltpu.make_async_remote_copy(
            src_ref=src, dst_ref=dst, send_sem=send, recv_sem=recv,
            device_id=(gx, gy), device_id_type=MESH,
        )

    def face_copy(step, link):
        _, where, here, there, _ = link
        return remote(
            fsend.at[step, rows_of(here, face), :],
            frecv.at[step, rows_of(there, face), :],
            f_ssem.at[step, here],
            f_rsem.at[step, there],
            *where,
        )

    def face_part(step, link, first, stop):
        _, where, here, there, _ = link
        size = face // 8

        def part_of(slot):
            start = slot * face + first * size
            if not isinstance(slot, int):
                start = pl.multiple_of(start, size)
            return pl.ds(start, (stop - first) * size)

        return remote(
            fsend.at[step, part_of(here), :],
            frecv.at[step, part_of(there), :],
            f_ssem.at[step, here],
            f_rsem.at[step, there],
            *where,
        )

    def send_part(step, stage, some):
        for link in some:
            for up, cuts in ((None, CUTS), (True, UP_CUTS), (False, DOWN_CUTS)):
                first, stop = cuts[stage], cuts[stage + 1]
                if first == stop or (up is None) != (link[4] is None):
                    continue
                side = True if up is None else link[4] if up else negate(link[4])
                when(both(link[0], side), face_part(step, link, first, stop).start)

    def edge_copy(link):
        _, where, here, there, _ = link
        return remote(
            esend.at[here], erecv.at[there], e_ssem.at[here], e_rsem.at[there], *where
        )

    def chain_copy(step, link):
        _, where, here, there, _ = link
        return remote(
            hsend.at[step], hrecv.at[step, there], h_ssem.at[step, here], h_rsem.at[step, there],
            *where,
        )

    def arrives(copy, link, cond=True):
        has, where, here, _, up = link
        when(both(has, cond), copy((has, where, here, here, up)).wait_recv)

    def comes_down(link):
        return True if link[4] is None else link[4]

    def goes_down(link):
        return True if link[4] is None else negate(link[4])

    lanes = 128

    def face_lines(slot):
        if nx == 2:
            number = 1 - a if isinstance(slot, int) and slot == 0 else slot + 1
        else:
            number = slot
        return rows_v[:, rows_of(number, face)].astype(F32)

    def build_face(slot):
        column = jnp.transpose(jnp.broadcast_to(face_lines(slot), (lanes, face)))
        for t in range(unknowns // lanes):
            cols = lax.broadcasted_iota(jnp.int32, (face, lanes), 1) + t * lanes
            perm[rows_of(slot, face), t * lanes : (t + 1) * lanes] = jnp.where(
                column == cols.astype(F32), 1.0, 0.0
            ).astype(BF16)

    def take_faces(step, field, some):
        for link in some:

            @apart
            def _(at=rows_of(link[2], face)):
                picks = perm[at, :]
                fsend[step, at, :] = dot(picks, field[0]) + dot(picks, field[1])

    smalls[0].wait()
    for slot in range(slots):
        build_face(slot)
    loads[0].wait()
    for load in loads[1:]:
        load.start()
    field = split(r_buf[...])
    take_faces(0, field, links[:1])
    pl.semaphore_wait(barrier, count)
    when(links[0][0], face_copy(0, links[0]).start)
    for link in links[1:]:
        take_faces(0, field, [link])
        when(link[0], face_copy(0, link).start)
    if nz > 1:
        line_round(0)

    along = [(z + dy) % ny for dy in range(ny)]

    def coarse_far(dy):
        return remote(
            c_all.at[g], c_all.at[g], cf_ssem.at[dy], c_rsem.at[g],
            a, member(team, along[dy] * 2 + core),
        )

    def coarse_near(dy):
        which = along[dy] * 2 + core
        return remote(
            c_all.at[which], c_all.at[which], cp_ssem.at[dy], c_rsem.at[which], a, partner
        )

    def coarse_arrived(which):
        remote(
            c_all.at[which], c_all.at[which], cp_ssem.at[0], c_rsem.at[which], a, partner
        ).wait_recv()

    loads[1].wait()
    coarse_near(0).start()
    for dy in range(1, ny):
        coarse_far(dy).start()

    for link in links[:-1]:
        if link[0] is not True:

            @pl.when(jnp.logical_not(link[0]))
            def _(link=link):
                here = link[2]
                for step in range(STEPS):
                    frecv[step, rows_of(here, face), :] = jnp.zeros((face, width), F32)
                erecv[here] = jnp.zeros(erecv.shape[1:], F32)
                for step in range(STEPS - 1):
                    hrecv[step, here] = jnp.zeros((prims, width), F32)

    lines = jnp.concatenate([face_lines(slot) for slot in range(slots)], axis=1)

    def build_t(i, carry):
        at = rows_of(i, block)
        here = lax.broadcasted_iota(jnp.int32, (block, slots * face), 0) + i * block
        perm_t[at, :] = jnp.where(here.astype(F32) == lines, 1.0, 0.0).astype(BF16)
        return carry

    lax.fori_loop(0, blocks, build_t, 0)

    smalls[1].wait()
    smalls[2].wait()
    eye = lax.broadcasted_iota(jnp.int32, (prims, prims), 0) == lax.broadcasted_iota(
        jnp.int32, (prims, prims), 1
    )
    prim_row = prim_v[...].astype(F32)
    prim_col = jnp.sum(jnp.where(eye, prim_row, 0.0), axis=1, keepdims=True)
    rate = jnp.sum(jnp.where(eye, decay_v[...], 0.0), axis=1, keepdims=True)
    pick_t = jnp.where(
        prim_col == lax.broadcasted_iota(jnp.int32, (prims, unknowns), 1).astype(F32), 1.0, 0.0
    ).astype(BF16)
    thrice = jnp.concatenate([prim_row] * 3, axis=1)
    tops = lax.broadcasted_iota(jnp.int32, (unknowns, 3 * prims), 0).astype(F32) == thrice
    high_side = lax.broadcasted_iota(jnp.int32, (unknowns, 3 * prims), 1) < 2 * prims
    pick_h = jnp.where(jnp.logical_and(tops, high_side), 1.0, 0.0).astype(BF16)
    pick_l = jnp.where(
        jnp.logical_and(tops, jnp.logical_not(high_side)), 1.0, 0.0
    ).astype(BF16)
    loads[2].wait()

    def halve(i, carry):
        at = rows_of(i, block)
        nh[at, :], nl[at, :] = split(n_buf[at, :])
        return carry

    lax.fori_loop(0, blocks, halve, 0)
    advance()
    sel[0:prims, :] = dot(pick_t, nh[...]).astype(BF16)
    sel[prims : 2 * prims, :] = dot(pick_t, nl[...]).astype(BF16)
    advance()
    npp[...] = dot(sel[...], perm_t[...]).astype(BF16)
    base[...] = stacked3(sel[...], field)
    advance()
    loads[3].wait()

    def halve_pick(i, carry):
        at = rows_of(i, block)
        high, low = split(d_buf[at, :])
        dh[at, :] = high
        dl[at, :] = low
        thin_ref[at, :] = (dot(high, pick_h) + dot(low, pick_l)).astype(BF16)
        return carry

    lax.fori_loop(0, blocks, halve_pick, 0)
    for _ in range(nz):
        advance()
    lifted = dot(perm[...], thin_ref[...])
    lifted = lifted[:, :prims] + lifted[:, 2 * prims :]
    for slot in range(slots):
        esend[slot] = pack(lifted[slot * face : (slot + 1) * face], 128 // prims)
    for link in links:
        when(link[0], edge_copy(link).start)

    order = [
        (dz, d)
        for dz in sorted(range(nz), key=lambda dz: -min(dz, nz - dz))
        for d in range(ng)
        if (dz, d) != (0, 0)
    ]

    def spread(step, dz, d):
        return remote(
            psend.at[step, mate_at[d]],
            gath.at[step, me],
            a_ssem.at[step],
            g_rsem.at[step],
            a,
            member((team + dz) % nz, mate_at[d]),
        )

    def all_spread(step):
        every = gath.at[step, pl.ds(0, ny_all - 1)]
        return remote(every, every, a_ssem.at[step], g_rsem.at[step], a, partner)

    def q_copy(step, d):
        return remote(
            qsend.at[step, mate_at[d]], cown.at[step, g], q_ssem.at[step], q_rsem.at[step],
            a, mates[d],
        )

    def first_copy(step, d):
        return remote(
            qsend.at[step, mate_at[d]], cprev.at[step, g], p_ssem.at[step], p_rsem.at[step],
            a + 1, mates[d],
        )

    def next_copy(step, q):
        return remote(
            csend.at[step, q], cprev.at[step, q], p_ssem.at[step], p_rsem.at[step],
            a + 1, me,
        )

    def all_q(step):
        every = cown.at[step, pl.ds(0, ng - 1)]
        return remote(every, every, q_ssem.at[step], q_rsem.at[step], a, partner)

    def all_p(step):
        every = cprev.at[step]
        return remote(every, every, p_ssem.at[step], p_rsem.at[step], a, partner)

    starts = jnp.logical_and(a == 0, a < nx - 1)
    passes = jnp.logical_and(a > 0, a < nx - 1)

    def sent_later(step):
        if step == 0:
            coarse_near(0).wait_send()
            for dy in range(1, ny):
                coarse_far(dy).wait_send()
                coarse_near(dy).wait_send()
            for link in links:
                when(link[0], edge_copy(link).wait_send)
                when(link[0], face_copy(0, link).wait_send)
        if step + 1 < STEPS:
            for link in links:
                when(link[0], face_copy(step + 1, link).wait_send)
                when(both(link[0], goes_down(link)), chain_copy(step, link).wait_send)
        all_q(step).wait_send()
        pl.when(a < nx - 1)(all_p(step).wait_send)

    for step in range(STEPS):
        last = step + 1 == STEPS
        if step == 0:
            arrives(functools.partial(face_copy, step), links[-1])
            inner = pl.ds(pl.multiple_of(in_slot * face, face), face)
            ghost = split(frecv[step, inner, :])

            def start_fill(i, carry, ghost=ghost, inner=inner):
                at = rows_of(i, block)
                back = perm_t[at, inner]
                jump[at, :] = r_buf[at, :] - dot(back, ghost[0]) - dot(back, ghost[1])
                return carry

            lax.fori_loop(0, blocks, start_fill, 0)
            for link in links[:-1]:
                arrives(functools.partial(face_copy, step), link)

            @apart
            def _(step=step):
                base[...] -= stacked3(npp[...], split(frecv[step]))

            prim = base[...]
        else:
            for link in links:
                arrives(functools.partial(face_copy, step), link)

            @apart
            def _(step=step):
                base[...] -= stacked3(npp[...], split(frecv[step]))

            for link in links:
                arrives(functools.partial(chain_copy, step - 1), link, comes_down(link))
            beside = jnp.concatenate([tall3(hrecv[step - 1, slot]) for slot in range(slots)])
            prim = base[...] + dot(couple[...], beside)
        for q in range(ng):
            psend[step, q] = pack(prim[:, q * part : (q + 1) * part])
        for dz, d in order:
            spread(step, dz, d).start()
        gath[step, me] = psend[step, g]
        if step == 0:
            outer = pl.ds(pl.multiple_of(out_slot * face, face), face)
            sides = [(pl.ds(slot * face, face)) for slot in range(xs)] + [outer]
            ghosts = [split(frecv[step, side, :]) for side in sides]
        else:
            for slot in range(slots):
                at = slice(slot * face, (slot + 1) * face)
                fix[at, :] = frecv[step, at, :] - 0.5 * dot(
                    edges[at, :], beside[slot * 3 * prims : (slot + 1) * 3 * prims]
                )
            sides = [pl.ds(0, slots * face)]
            ghosts = [split(fix[...])]

        def fill(i, carry, step=step, sides=sides, ghosts=ghosts):
            at = rows_of(i, block)
            value = jump[at, :] if step == 0 else t2_ref[at, :]
            for side, ghost in zip(sides, ghosts):
                back = perm_t[at, side]
                value = value - dot(back, ghost[0]) - dot(back, ghost[1])
            jump[at, :] = value
            high_v[at, :], low_v[at, :] = split(value)
            return carry

        lax.fori_loop(0, blocks, fill, 0)

        def multiply(i, carry):
            at = rows_of(i, block)
            work = dot3((nh[at, :], nl[at, :]), (high_v[...], low_v[...]))
            high_w[at, :], low_w[at, :] = split(work)
            return carry

        lax.fori_loop(0, blocks, multiply, 0)
        if step == 0:
            for dy in range(1, ny):
                coarse_arrived(along[dy] * 2 + core)
                coarse_near(dy).start()

        def smooth(i, carry, step=step, last=last):
            at = rows_of(i, block)
            update = dot3((dh[at, :], dl[at, :]), (high_w[...], low_w[...]))
            if step == 0:
                t1_ref[at, :] = update
            else:
                t1_ref[at, :] += update
            rest = jump[at, :] - 0.5 * update
            t2_ref[at, :] = rest
            if not last:
                high_v[at, :], low_v[at, :] = split(rest)
            return carry

        lax.fori_loop(0, blocks, smooth, 0)
        if not last:
            rests = (high_v[...], low_v[...])
            for link in links[:-1]:
                take_faces(step + 1, rests, [link])
                send_part(step + 1, 0, [link])
            take_faces(step + 1, rests, links[-1:])
            face_copy(step + 1, links[-1]).start()
        if step == 0:
            for dy in range(ny):
                coarse_arrived(along[dy] * 2 + 1 - core)
            size = ng * prims
            cs[0:size, :], cs[size : 2 * size, :] = split(
                c_all[...].reshape(size, c_all.shape[2])
            )
        if step > 0:
            sent_later(step - 1)
        all_spread(step).wait_recv()

        @apart
        def _(step=step):
            values = jnp.concatenate([unpack(gath[step, b]) for b in range(ny_all)], axis=0)
            quarter = stacked3(cs[...], split(values))
            for q in range(ng):
                qsend[step, q] = pack(quarter[q * prims : (q + 1) * prims, :])

        @pl.when(starts)
        def _(step=step):
            for d in range(ng):
                first_copy(step, d).start()

        for d in range(1, ng):
            q_copy(step, d).start()
        if not last:
            send_part(step + 1, 1, links[:-1])
        cown[step, g] = qsend[step, g]
        all_spread(step).wait_send()
        all_q(step).wait_recv()

        def joined(ref, step=step):
            return jnp.concatenate([unpack(ref[step, q]) for q in range(ng)], axis=1)

        @pl.when(a == 0)
        def _(step=step):
            chain_v[...] = joined(cown)

        @pl.when(a > 0)
        def _(step=step):
            all_p(step).wait_recv()
            chain_v[...] = joined(cown) + rate * joined(cprev)

        @pl.when(passes)
        def _(step=step):
            for q in range(ng):
                csend[step, q] = pack(chain_v[:, q * part : (q + 1) * part])
                next_copy(step, q).start()

        if last:
            last_ref[...] = chain_v[...]
        else:
            hsend[step] = chain_v[...]
            for link in links:
                when(both(link[0], goes_down(link)), chain_copy(step, link).start)
            send_part(step + 1, 2, links[:-1])
            if nx > 1:

                @pl.when(a > 0)
                def _(step=step):
                    hrecv[step, 0] = joined(cprev)

            chain = tall3(chain_v[...])

            def finish(i, carry, chain=chain):
                at = rows_of(i, block)
                more = dot(thin_ref[at, :], chain)
                t1_ref[at, :] += more
                t2_ref[at, :] -= 0.5 * more
                return carry

            lax.fori_loop(0, blocks, finish, 0)
            base[...] = stacked3(sel[...], split(t2_ref[...]))
            if step == 0:
                for link in links:
                    arrives(edge_copy, link)
                for slot in range(slots):
                    at = slice(slot * face, (slot + 1) * face)
                    high, low = split(unpack(erecv[slot], prims))
                    edges[at, :] = jnp.concatenate([high, high, low], axis=1)
                    both_ways = dot(npp[:, at], edges[at, :])
                    across = both_ways[:prims, :prims] + both_ways[:prims, 2 * prims :]
                    high, low = split(0.5 * (across + both_ways[prims:, :prims]))
                    for k, piece_of in enumerate((high, high, low)):
                        left = (3 * slot + k) * prims
                        couple[:, left : left + prims] = piece_of
    sent_later(STEPS - 1)


def closing(t1, t2, thin, chain, sol, res):
    rows = sol.shape[0]
    at = pl.ds(pl.multiple_of(pl.program_id(0) * rows, rows), rows)
    more = dot(thin[at, :], tall3(chain[...]))
    sol[...] = t1[at, :] + more
    res[...] = t2[at, :] - 0.5 * more


def local(nx, ny_all, residual_in, neumann, dirichlet, coarse, decay, face_rows, primal):
    unknowns, width = residual_in.shape[2:]
    prims = primal.shape[2]
    order = coarse.shape[2]
    nz, ny = line_sizes(ny_all)
    ng = 2 * ny
    part = width // ng
    fold = max(1, 128 // part)
    piece = (prims // fold, fold * part)
    face = unknowns // 4
    slots = x_slots(nx) + 2
    anywhere = pl.BlockSpec(memory_space=pl.ANY)
    inside = pl.BlockSpec(memory_space=pltpu.VMEM)
    square = (unknowns, unknowns)
    field = (unknowns, width)
    ghosts = (slots * face, width)
    edge = (slots, face * prims // 128, 128)
    dma = pltpu.SemaphoreType.DMA
    whole = jax.ShapeDtypeStruct(field, F32)
    outs = [(field, F32), (field, F32), ((unknowns, 3 * prims), BF16), ((prims, width), F32)]
    pieces = pl.pallas_call(
        functools.partial(kernel, nx, ny_all),
        out_shape=tuple(pltpu.VMEM(shape, kind) for shape, kind in outs),
        in_specs=[anywhere] * 7,
        out_specs=(inside,) * 4,
        scratch_shapes=[
            pltpu.VMEM(square, F32),
            pltpu.VMEM(square, F32),
        ]
        + [pltpu.VMEM(square, BF16)] * 4
        + [
            pltpu.VMEM((slots * face, unknowns), BF16),
            pltpu.VMEM((unknowns, slots * face), BF16),
        ]
        + [pltpu.VMEM(field, F32)] * 2
        + [pltpu.VMEM(field, BF16)] * 4
        + [
            pltpu.VMEM((STEPS,) + ghosts, F32),
            pltpu.VMEM((STEPS,) + ghosts, F32),
            pltpu.VMEM(ghosts, F32),
            pltpu.VMEM((ng, prims, order), F32),
            pltpu.VMEM((2 * ng * prims, order), BF16),
            pltpu.VMEM((STEPS, ng) + piece, F32),
            pltpu.VMEM((STEPS, ny_all) + piece, F32),
            pltpu.VMEM((STEPS, ng) + piece, F32),
            pltpu.VMEM((STEPS, ng) + piece, F32),
            pltpu.VMEM((STEPS, ng) + piece, F32),
            pltpu.VMEM((STEPS, ng) + piece, F32),
            pltpu.VMEM((2 * prims, unknowns), BF16),
            pltpu.VMEM((2 * prims, slots * face), BF16),
            pltpu.VMEM((prims, width), F32),
            pltpu.VMEM((1, prims), F32),
            pltpu.VMEM((1, unknowns), jnp.int32),
            pltpu.VMEM((1, prims), jnp.int32),
            pltpu.VMEM(edge, F32),
            pltpu.VMEM(edge, F32),
            pltpu.VMEM((slots * face, 3 * prims), BF16),
            pltpu.VMEM((prims, slots * 3 * prims), BF16),
            pltpu.VMEM((prims, width), F32),
            pltpu.VMEM((STEPS - 1, prims, width), F32),
            pltpu.VMEM((STEPS - 1, slots, prims, width), F32),
            dma((4,)),
            dma((3,)),
            dma((ny,)),
            dma((ny,)),
            dma((ng,)),
            dma((STEPS, slots)),
            dma((STEPS, slots)),
            dma((STEPS,)),
            dma((STEPS,)),
            dma((STEPS,)),
            dma((STEPS,)),
            dma((STEPS,)),
            dma((STEPS,)),
            dma((slots,)),
            dma((slots,)),
            dma((STEPS - 1, slots)),
            dma((STEPS - 1, slots)),
            pltpu.SemaphoreType.REGULAR((max(1, nz - 1), 2)),
        ],
        compiler_params=pltpu.CompilerParams(
            collective_id=0, has_side_effects=True, vmem_limit_bytes=62720 * 1024
        ),
    )(
        residual_in[0, 0],
        neumann[0, 0],
        dirichlet[0, 0],
        coarse[0],
        decay[0],
        face_rows[0],
        primal[0],
    )
    rows = unknowns // 2
    tall = pl.BlockSpec((rows, width), lambda i: (i, 0))
    sol, res = pl.pallas_call(
        closing,
        grid=(unknowns // rows,),
        out_shape=(whole, whole),
        in_specs=[inside] * 4,
        out_specs=(tall, tall),
        compiler_params=pltpu.CompilerParams(vmem_limit_bytes=16000 * 1024),
    )(*pieces)
    return (sol[None, None], res[None, None])


def solution(mesh):
    return jax.shard_map(
        functools.partial(local, mesh.shape["gx"], mesh.shape["gy"]),
        mesh=mesh,
        in_specs=(
            P("gx", "gy", None, None),
            P("gx", "gy", None, None),
            P("gx", "gy", None, None),
            P("gx", "gy", None),
            P("gx", "gy", None),
            P("gx", "gy", None),
            P("gx", "gy", None),
        ),
        out_specs=(P("gx", "gy", None, None), P("gx", "gy", None, None)),
        check_vma=False,
    )
```

```python
import functools

import jax
import jax.numpy as jnp
from jax import lax
from jax.experimental import pallas as pl
from jax.experimental.pallas import tpu as pltpu
from jax.sharding import PartitionSpec as P

STEPS = 2
CUTS = (0, 4, 8, 8)
UP_CUTS = (0, 2, 8, 8)
DOWN_CUTS = (0, 8, 8, 8)
MESH = pl.DeviceIdType.MESH
F32 = jnp.float32
BF16 = jnp.bfloat16


def dot(a, b):
    return jnp.dot(a, b, preferred_element_type=F32)


def split(x):
    high = x.astype(BF16)
    return high, (x - high.astype(F32)).astype(BF16)


def dot3(a, b):
    return dot(a[0], b[0]) + dot(a[0], b[1]) + dot(a[1], b[0])


def stacked3(a, b):
    rows = a.shape[0] // 2
    first = dot(a, b[0])
    return first[:rows] + first[rows:] + dot(a[:rows], b[1])


def tall3(x):
    high, low = split(x)
    return jnp.concatenate([high, low, high], axis=0)


def when(cond, body):
    if cond is True:
        body()
    elif cond is not False:
        pl.when(cond)(body)


def both(p, q):
    if p is True or q is False:
        return q
    if q is True or p is False:
        return p
    return jnp.logical_and(p, q)


def negate(p):
    return not p if isinstance(p, bool) else jnp.logical_not(p)


def line_sizes(count):
    chips = count // 2
    inner = 1
    while inner * inner * 4 <= chips:
        inner *= 2
    return chips // inner, inner


def x_slots(nx):
    return 1 if nx == 2 else 2


def kernel(
    nx, ny_all, r_hbm, n_hbm, d_hbm, c_hbm, decay_hbm, rows_hbm, prim_hbm,
    t1_ref, t2_ref, thin_ref, last_ref,
    n_buf, d_buf, nh, nl, dh, dl, perm, perm_t,
    r_buf, jump, high_v, low_v, high_w, low_w, fsend, frecv, fix, c_all, cs, psend, gath, qsend, cown, cprev, csend,
    sel, npp, base, decay_v, rows_v, prim_v, esend, erecv, edges, couple, chain_v, hsend, hrecv,
    load_sem, small_sem, cf_ssem, cp_ssem, c_rsem, f_ssem, f_rsem, a_ssem, g_rsem,
    q_ssem, q_rsem, p_ssem, p_rsem, e_ssem, e_rsem, h_ssem, h_rsem, line_sem,
):
    unknowns, width = r_buf.shape
    face = unknowns // 4
    prims = c_all.shape[1]
    nz, ny = line_sizes(ny_all)
    ng = 2 * ny
    part = width // ng
    fold = max(1, 128 // part)
    short = prims // fold
    block = 2 * face
    blocks = unknowns // block
    xs = x_slots(nx)
    slots = xs + 2

    a = lax.axis_index("gx")
    me = lax.axis_index("gy")
    plane = 2 * ny
    core = me % 2
    y = me // 2 % ny
    z = me // plane
    partner = me + 1 - 2 * core

    team = z // ny * ny + y
    g = z % ny * 2 + core

    def member(which, j):
        return ((which // ny * ny + j // 2) * ny + which % ny) * 2 + j % 2

    smalls = [
        pltpu.make_async_copy(src, dst, small_sem.at[i])
        for i, (src, dst) in enumerate(
            [(rows_hbm, rows_v), (prim_hbm, prim_v), (decay_hbm, decay_v)]
        )
    ]
    loads = [
        pltpu.make_async_copy(src, dst, load_sem.at[i])
        for i, (src, dst) in enumerate(
            [(r_hbm, r_buf), (c_hbm, c_all.at[g]), (n_hbm, n_buf), (d_hbm, d_buf)]
        )
    ]
    smalls[0].start()
    loads[0].start()
    smalls[1].start()
    smalls[2].start()

    barrier = pltpu.get_barrier_semaphore()

    def greet(gx, gy):
        pl.semaphore_signal(barrier, inc=1, device_id=(gx, gy), device_id_type=MESH)

    out_slot = xs + core
    in_slot = xs + 1 - core
    outward = me - 1 + 2 * core
    has_out = jnp.logical_and(outward >= 0, outward < ny_all)
    links = [(has_out, (a, outward), out_slot, in_slot, None)]
    if nx == 2:
        links.append((True, (1 - a, me), 0, 0, a == 0))
    else:
        links.append((a > 0, (a - 1, me), 0, 1, False))
        links.append((a < nx - 1, (a + 1, me), 1, 0, True))
    links.append((True, (a, partner), in_slot, out_slot, None))
    mate_at = [
        (z + dz) % ny * 2 + (core + dc) % 2
        for dz, dc in [(0, 0)] + [(k, c) for k in range(1, ny) for c in range(2)] + [(0, 1)]
    ]
    mates = [member(team, j) for j in mate_at]
    below, above = z > 0, z < nz - 1
    count = jnp.int32(ng - 1 + plane - 1)
    for has, where, _, _, _ in links[:-1]:
        when(has, functools.partial(greet, *where))
        count = count + (1 if has is True else has.astype(jnp.int32))
    for d in range(1, ng):
        greet(a, mates[d])
    for d in range(1, plane):
        greet(a, z * plane + (me + d) % plane)
    pl.when(below)(functools.partial(greet, a, me - plane))
    pl.when(above)(functools.partial(greet, a, me + plane))
    count = count + below.astype(jnp.int32) + above.astype(jnp.int32)
    if nx > 1:

        @pl.when(a < 2)
        def _():
            for d in range(1, ng):
                greet(1 - a, mates[d])

        count = count + (a < 2).astype(jnp.int32) * (ng - 1)

    def line_round(turn):
        def tell(low):
            pl.semaphore_signal(
                line_sem.at[turn, 1 if low else 0],
                inc=1,
                device_id=(a, me - plane if low else me + plane),
                device_id_type=MESH,
            )

        pl.when(below)(functools.partial(tell, True))
        pl.when(above)(functools.partial(tell, False))

    def line_wait(turn):
        pl.when(below)(lambda: pl.semaphore_wait(line_sem.at[turn, 0], 1))
        pl.when(above)(lambda: pl.semaphore_wait(line_sem.at[turn, 1], 1))

    turns = [0]

    def advance():
        turn = turns[0]
        if turn < nz - 1:
            line_wait(turn)
            if turn + 1 < nz - 1:
                line_round(turn + 1)
            turns[0] = turn + 1

    def pack(x, pieces=fold):
        size = x.shape[0] // pieces
        return jnp.concatenate([x[j * size : (j + 1) * size] for j in range(pieces)], axis=1)

    def unpack(x, columns=part):
        return jnp.concatenate(
            [x[:, j * columns : (j + 1) * columns] for j in range(x.shape[1] // columns)], axis=0
        )

    apart = pl.when(a >= 0)

    def rows_of(i, size):
        if isinstance(i, int):
            return pl.ds(i * size, size)
        return pl.ds(pl.multiple_of(i * size, size), size)

    def remote(src, dst, send, recv, gx, gy):
        return pltpu.make_async_remote_copy(
            src_ref=src, dst_ref=dst, send_sem=send, recv_sem=recv,
            device_id=(gx, gy), device_id_type=MESH,
        )

    def face_copy(step, link):
        _, where, here, there, _ = link
        return remote(
            fsend.at[step, rows_of(here, face), :],
            frecv.at[step, rows_of(there, face), :],
            f_ssem.at[step, here],
            f_rsem.at[step, there],
            *where,
        )

    def face_part(step, link, first, stop):
        _, where, here, there, _ = link
        size = face // 8

        def part_of(slot):
            start = slot * face + first * size
            if not isinstance(slot, int):
                start = pl.multiple_of(start, size)
            return pl.ds(start, (stop - first) * size)

        return remote(
            fsend.at[step, part_of(here), :],
            frecv.at[step, part_of(there), :],
            f_ssem.at[step, here],
            f_rsem.at[step, there],
            *where,
        )

    def send_part(step, stage, some):
        for link in some:
            for up, cuts in ((None, CUTS), (True, UP_CUTS), (False, DOWN_CUTS)):
                first, stop = cuts[stage], cuts[stage + 1]
                if first == stop or (up is None) != (link[4] is None):
                    continue
                side = True if up is None else link[4] if up else negate(link[4])
                when(both(link[0], side), face_part(step, link, first, stop).start)

    def edge_copy(link):
        _, where, here, there, _ = link
        return remote(
            esend.at[here], erecv.at[there], e_ssem.at[here], e_rsem.at[there], *where
        )

    def chain_copy(step, link):
        _, where, here, there, _ = link
        return remote(
            hsend.at[step], hrecv.at[step, there], h_ssem.at[step, here], h_rsem.at[step, there],
            *where,
        )

    def arrives(copy, link, cond=True):
        has, where, here, _, up = link
        when(both(has, cond), copy((has, where, here, here, up)).wait_recv)

    def comes_down(link):
        return True if link[4] is None else link[4]

    def goes_down(link):
        return True if link[4] is None else negate(link[4])

    lanes = 128

    def face_lines(slot):
        if nx == 2:
            number = 1 - a if isinstance(slot, int) and slot == 0 else slot + 1
        else:
            number = slot
        return rows_v[:, rows_of(number, face)].astype(F32)

    def build_face(slot):
        column = jnp.transpose(jnp.broadcast_to(face_lines(slot), (lanes, face)))
        for t in range(unknowns // lanes):
            cols = lax.broadcasted_iota(jnp.int32, (face, lanes), 1) + t * lanes
            perm[rows_of(slot, face), t * lanes : (t + 1) * lanes] = jnp.where(
                column == cols.astype(F32), 1.0, 0.0
            ).astype(BF16)

    def take_faces(step, field, some):
        for link in some:

            @apart
            def _(at=rows_of(link[2], face)):
                picks = perm[at, :]
                fsend[step, at, :] = dot(picks, field[0]) + dot(picks, field[1])

    smalls[0].wait()
    for slot in range(slots):
        build_face(slot)
    loads[0].wait()
    for load in loads[1:]:
        load.start()
    field = split(r_buf[...])
    take_faces(0, field, links[:1])
    pl.semaphore_wait(barrier, count)
    when(links[0][0], face_copy(0, links[0]).start)
    for link in links[1:]:
        take_faces(0, field, [link])
        when(link[0], face_copy(0, link).start)
    if nz > 1:
        line_round(0)

    along = [(z + dy) % ny for dy in range(ny)]

    def coarse_far(dy):
        return remote(
            c_all.at[g], c_all.at[g], cf_ssem.at[dy], c_rsem.at[g],
            a, member(team, along[dy] * 2 + core),
        )

    def coarse_near(dy):
        which = along[dy] * 2 + core
        return remote(
            c_all.at[which], c_all.at[which], cp_ssem.at[dy], c_rsem.at[which], a, partner
        )

    def coarse_arrived(which):
        remote(
            c_all.at[which], c_all.at[which], cp_ssem.at[0], c_rsem.at[which], a, partner
        ).wait_recv()

    loads[1].wait()
    coarse_near(0).start()
    for dy in range(1, ny):
        coarse_far(dy).start()

    for link in links[:-1]:
        if link[0] is not True:

            @pl.when(jnp.logical_not(link[0]))
            def _(link=link):
                here = link[2]
                for step in range(STEPS):
                    frecv[step, rows_of(here, face), :] = jnp.zeros((face, width), F32)
                erecv[here] = jnp.zeros(erecv.shape[1:], F32)
                for step in range(STEPS - 1):
                    hrecv[step, here] = jnp.zeros((prims, width), F32)

    lines = jnp.concatenate([face_lines(slot) for slot in range(slots)], axis=1)

    def build_t(i, carry):
        at = rows_of(i, block)
        here = lax.broadcasted_iota(jnp.int32, (block, slots * face), 0) + i * block
        perm_t[at, :] = jnp.where(here.astype(F32) == lines, 1.0, 0.0).astype(BF16)
        return carry

    lax.fori_loop(0, blocks, build_t, 0)

    smalls[1].wait()
    smalls[2].wait()
    eye = lax.broadcasted_iota(jnp.int32, (prims, prims), 0) == lax.broadcasted_iota(
        jnp.int32, (prims, prims), 1
    )
    prim_row = prim_v[...].astype(F32)
    prim_col = jnp.sum(jnp.where(eye, prim_row, 0.0), axis=1, keepdims=True)
    rate = jnp.sum(jnp.where(eye, decay_v[...], 0.0), axis=1, keepdims=True)
    pick_t = jnp.where(
        prim_col == lax.broadcasted_iota(jnp.int32, (prims, unknowns), 1).astype(F32), 1.0, 0.0
    ).astype(BF16)
    thrice = jnp.concatenate([prim_row] * 3, axis=1)
    tops = lax.broadcasted_iota(jnp.int32, (unknowns, 3 * prims), 0).astype(F32) == thrice
    high_side = lax.broadcasted_iota(jnp.int32, (unknowns, 3 * prims), 1) < 2 * prims
    pick_h = jnp.where(jnp.logical_and(tops, high_side), 1.0, 0.0).astype(BF16)
    pick_l = jnp.where(
        jnp.logical_and(tops, jnp.logical_not(high_side)), 1.0, 0.0
    ).astype(BF16)
    loads[2].wait()

    def halve(i, carry):
        at = rows_of(i, block)
        nh[at, :], nl[at, :] = split(n_buf[at, :])
        return carry

    lax.fori_loop(0, blocks, halve, 0)
    advance()
    sel[0:prims, :] = dot(pick_t, nh[...]).astype(BF16)
    sel[prims : 2 * prims, :] = dot(pick_t, nl[...]).astype(BF16)
    advance()
    npp[...] = dot(sel[...], perm_t[...]).astype(BF16)
    base[...] = stacked3(sel[...], field)
    advance()
    loads[3].wait()

    def halve_pick(i, carry):
        at = rows_of(i, block)
        high, low = split(d_buf[at, :])
        dh[at, :] = high
        dl[at, :] = low
        thin_ref[at, :] = (dot(high, pick_h) + dot(low, pick_l)).astype(BF16)
        return carry

    lax.fori_loop(0, blocks, halve_pick, 0)
    for _ in range(nz):
        advance()
    lifted = dot(perm[...], thin_ref[...])
    lifted = lifted[:, :prims] + lifted[:, 2 * prims :]
    for slot in range(slots):
        esend[slot] = pack(lifted[slot * face : (slot + 1) * face], 128 // prims)
    for link in links:
        when(link[0], edge_copy(link).start)

    order = [
        (dz, d)
        for dz in sorted(range(nz), key=lambda dz: -min(dz, nz - dz))
        for d in range(ng)
        if (dz, d) != (0, 0)
    ]

    def spread(step, dz, d):
        return remote(
            psend.at[step, mate_at[d]],
            gath.at[step, me],
            a_ssem.at[step],
            g_rsem.at[step],
            a,
            member((team + dz) % nz, mate_at[d]),
        )

    def all_spread(step):
        every = gath.at[step, pl.ds(0, ny_all - 1)]
        return remote(every, every, a_ssem.at[step], g_rsem.at[step], a, partner)

    def q_copy(step, d):
        return remote(
            qsend.at[step, mate_at[d]], cown.at[step, g], q_ssem.at[step], q_rsem.at[step],
            a, mates[d],
        )

    def first_copy(step, d):
        return remote(
            qsend.at[step, mate_at[d]], cprev.at[step, g], p_ssem.at[step], p_rsem.at[step],
            a + 1, mates[d],
        )

    def next_copy(step, q):
        return remote(
            csend.at[step, q], cprev.at[step, q], p_ssem.at[step], p_rsem.at[step],
            a + 1, me,
        )

    def all_q(step):
        every = cown.at[step, pl.ds(0, ng - 1)]
        return remote(every, every, q_ssem.at[step], q_rsem.at[step], a, partner)

    def all_p(step):
        every = cprev.at[step]
        return remote(every, every, p_ssem.at[step], p_rsem.at[step], a, partner)

    starts = jnp.logical_and(a == 0, a < nx - 1)
    passes = jnp.logical_and(a > 0, a < nx - 1)

    def sent_later(step):
        if step == 0:
            coarse_near(0).wait_send()
            for dy in range(1, ny):
                coarse_far(dy).wait_send()
                coarse_near(dy).wait_send()
            for link in links:
                when(link[0], edge_copy(link).wait_send)
                when(link[0], face_copy(0, link).wait_send)
        if step + 1 < STEPS:
            for link in links:
                when(link[0], face_copy(step + 1, link).wait_send)
                when(both(link[0], goes_down(link)), chain_copy(step, link).wait_send)
        all_q(step).wait_send()
        pl.when(a < nx - 1)(all_p(step).wait_send)

    for step in range(STEPS):
        last = step + 1 == STEPS
        if step == 0:
            arrives(functools.partial(face_copy, step), links[-1])
            inner = pl.ds(pl.multiple_of(in_slot * face, face), face)
            ghost = split(frecv[step, inner, :])

            def start_fill(i, carry, ghost=ghost, inner=inner):
                at = rows_of(i, block)
                back = perm_t[at, inner]
                jump[at, :] = r_buf[at, :] - dot(back, ghost[0]) - dot(back, ghost[1])
                return carry

            lax.fori_loop(0, blocks, start_fill, 0)
            for link in links[:-1]:
                arrives(functools.partial(face_copy, step), link)

            @apart
            def _(step=step):
                base[...] -= stacked3(npp[...], split(frecv[step]))

            prim = base[...]
        else:
            for link in links:
                arrives(functools.partial(face_copy, step), link)

            @apart
            def _(step=step):
                base[...] -= stacked3(npp[...], split(frecv[step]))

            for link in links:
                arrives(functools.partial(chain_copy, step - 1), link, comes_down(link))
            beside = jnp.concatenate([tall3(hrecv[step - 1, slot]) for slot in range(slots)])
            prim = base[...] + dot(couple[...], beside)
        for q in range(ng):
            psend[step, q] = pack(prim[:, q * part : (q + 1) * part])
        for dz, d in order:
            spread(step, dz, d).start()
        gath[step, me] = psend[step, g]
        if step == 0:
            outer = pl.ds(pl.multiple_of(out_slot * face, face), face)
            sides = [(pl.ds(slot * face, face)) for slot in range(xs)] + [outer]
            ghosts = [split(frecv[step, side, :]) for side in sides]
        else:
            for slot in range(slots):
                at = slice(slot * face, (slot + 1) * face)
                fix[at, :] = frecv[step, at, :] - 0.5 * dot(
                    edges[at, :], beside[slot * 3 * prims : (slot + 1) * 3 * prims]
                )
            sides = [pl.ds(0, slots * face)]
            ghosts = [split(fix[...])]

        def fill(i, carry, step=step, sides=sides, ghosts=ghosts):
            at = rows_of(i, block)
            value = jump[at, :] if step == 0 else t2_ref[at, :]
            for side, ghost in zip(sides, ghosts):
                back = perm_t[at, side]
                value = value - dot(back, ghost[0]) - dot(back, ghost[1])
            jump[at, :] = value
            high_v[at, :], low_v[at, :] = split(value)
            return carry

        lax.fori_loop(0, blocks, fill, 0)

        def multiply(i, carry):
            at = rows_of(i, block)
            work = dot3((nh[at, :], nl[at, :]), (high_v[...], low_v[...]))
            high_w[at, :], low_w[at, :] = split(work)
            return carry

        lax.fori_loop(0, blocks, multiply, 0)
        if step == 0:
            for dy in range(1, ny):
                coarse_arrived(along[dy] * 2 + core)
                coarse_near(dy).start()

        def smooth(i, carry, step=step, last=last):
            at = rows_of(i, block)
            update = dot3((dh[at, :], dl[at, :]), (high_w[...], low_w[...]))
            if step == 0:
                t1_ref[at, :] = update
            else:
                t1_ref[at, :] += update
            rest = jump[at, :] - 0.5 * update
            t2_ref[at, :] = rest
            if not last:
                high_v[at, :], low_v[at, :] = split(rest)
            return carry

        lax.fori_loop(0, blocks, smooth, 0)
        if not last:
            rests = (high_v[...], low_v[...])
            for link in links[:-1]:
                take_faces(step + 1, rests, [link])
                send_part(step + 1, 0, [link])
            take_faces(step + 1, rests, links[-1:])
            face_copy(step + 1, links[-1]).start()
        if step == 0:
            for dy in range(ny):
                coarse_arrived(along[dy] * 2 + 1 - core)
            size = ng * prims
            cs[0:size, :], cs[size : 2 * size, :] = split(
                c_all[...].reshape(size, c_all.shape[2])
            )
        if step > 0:
            sent_later(step - 1)
        all_spread(step).wait_recv()

        @apart
        def _(step=step):
            values = jnp.concatenate([unpack(gath[step, b]) for b in range(ny_all)], axis=0)
            quarter = stacked3(cs[...], split(values))
            for q in range(ng):
                qsend[step, q] = pack(quarter[q * prims : (q + 1) * prims, :])

        @pl.when(starts)
        def _(step=step):
            for d in [*range(1, ng), 0]:
                first_copy(step, d).start()

        for d in range(1, ng):
            q_copy(step, d).start()
        if not last:
            send_part(step + 1, 1, links[:-1])
        cown[step, g] = qsend[step, g]
        all_spread(step).wait_send()
        all_q(step).wait_recv()

        def joined(ref, step=step):
            return jnp.concatenate([unpack(ref[step, q]) for q in range(ng)], axis=1)

        @pl.when(a == 0)
        def _(step=step):
            chain_v[...] = joined(cown)

        @pl.when(a > 0)
        def _(step=step):
            all_p(step).wait_recv()
            chain_v[...] = joined(cown) + rate * joined(cprev)

        @pl.when(passes)
        def _(step=step):
            for q in range(ng):
                csend[step, q] = pack(chain_v[:, q * part : (q + 1) * part])
                next_copy(step, q).start()

        if last:
            last_ref[...] = chain_v[...]
        else:
            hsend[step] = chain_v[...]
            for link in links:
                when(both(link[0], goes_down(link)), chain_copy(step, link).start)
            send_part(step + 1, 2, links[:-1])
            if nx > 1:

                @pl.when(a > 0)
                def _(step=step):
                    hrecv[step, 0] = joined(cprev)

            chain = tall3(chain_v[...])

            def finish(i, carry, chain=chain):
                at = rows_of(i, block)
                more = dot(thin_ref[at, :], chain)
                t1_ref[at, :] += more
                t2_ref[at, :] -= 0.5 * more
                return carry

            lax.fori_loop(0, blocks, finish, 0)
            base[...] = stacked3(sel[...], split(t2_ref[...]))
            if step == 0:
                for link in links:
                    arrives(edge_copy, link)
                for slot in range(slots):
                    at = slice(slot * face, (slot + 1) * face)
                    high, low = split(unpack(erecv[slot], prims))
                    edges[at, :] = jnp.concatenate([high, high, low], axis=1)
                    both_ways = dot(npp[:, at], edges[at, :])
                    across = both_ways[:prims, :prims] + both_ways[:prims, 2 * prims :]
                    high, low = split(0.5 * (across + both_ways[prims:, :prims]))
                    for k, piece_of in enumerate((high, high, low)):
                        left = (3 * slot + k) * prims
                        couple[:, left : left + prims] = piece_of
    sent_later(STEPS - 1)


def closing(t1, t2, thin, chain, sol, res):
    rows = sol.shape[0]
    at = pl.ds(pl.multiple_of(pl.program_id(0) * rows, rows), rows)
    more = dot(thin[at, :], tall3(chain[...]))
    sol[...] = t1[at, :] + more
    res[...] = t2[at, :] - 0.5 * more


def local(nx, ny_all, residual_in, neumann, dirichlet, coarse, decay, face_rows, primal):
    unknowns, width = residual_in.shape[2:]
    prims = primal.shape[2]
    order = coarse.shape[2]
    nz, ny = line_sizes(ny_all)
    ng = 2 * ny
    part = width // ng
    fold = max(1, 128 // part)
    piece = (prims // fold, fold * part)
    face = unknowns // 4
    slots = x_slots(nx) + 2
    anywhere = pl.BlockSpec(memory_space=pl.ANY)
    inside = pl.BlockSpec(memory_space=pltpu.VMEM)
    square = (unknowns, unknowns)
    field = (unknowns, width)
    ghosts = (slots * face, width)
    edge = (slots, face * prims // 128, 128)
    dma = pltpu.SemaphoreType.DMA
    whole = jax.ShapeDtypeStruct(field, F32)
    outs = [(field, F32), (field, F32), ((unknowns, 3 * prims), BF16), ((prims, width), F32)]
    pieces = pl.pallas_call(
        functools.partial(kernel, nx, ny_all),
        out_shape=tuple(pltpu.VMEM(shape, kind) for shape, kind in outs),
        in_specs=[anywhere] * 7,
        out_specs=(inside,) * 4,
        scratch_shapes=[
            pltpu.VMEM(square, F32),
            pltpu.VMEM(square, F32),
        ]
        + [pltpu.VMEM(square, BF16)] * 4
        + [
            pltpu.VMEM((slots * face, unknowns), BF16),
            pltpu.VMEM((unknowns, slots * face), BF16),
        ]
        + [pltpu.VMEM(field, F32)] * 2
        + [pltpu.VMEM(field, BF16)] * 4
        + [
            pltpu.VMEM((STEPS,) + ghosts, F32),
            pltpu.VMEM((STEPS,) + ghosts, F32),
            pltpu.VMEM(ghosts, F32),
            pltpu.VMEM((ng, prims, order), F32),
            pltpu.VMEM((2 * ng * prims, order), BF16),
            pltpu.VMEM((STEPS, ng) + piece, F32),
            pltpu.VMEM((STEPS, ny_all) + piece, F32),
            pltpu.VMEM((STEPS, ng) + piece, F32),
            pltpu.VMEM((STEPS, ng) + piece, F32),
            pltpu.VMEM((STEPS, ng) + piece, F32),
            pltpu.VMEM((STEPS, ng) + piece, F32),
            pltpu.VMEM((2 * prims, unknowns), BF16),
            pltpu.VMEM((2 * prims, slots * face), BF16),
            pltpu.VMEM((prims, width), F32),
            pltpu.VMEM((1, prims), F32),
            pltpu.VMEM((1, unknowns), jnp.int32),
            pltpu.VMEM((1, prims), jnp.int32),
            pltpu.VMEM(edge, F32),
            pltpu.VMEM(edge, F32),
            pltpu.VMEM((slots * face, 3 * prims), BF16),
            pltpu.VMEM((prims, slots * 3 * prims), BF16),
            pltpu.VMEM((prims, width), F32),
            pltpu.VMEM((STEPS - 1, prims, width), F32),
            pltpu.VMEM((STEPS - 1, slots, prims, width), F32),
            dma((4,)),
            dma((3,)),
            dma((ny,)),
            dma((ny,)),
            dma((ng,)),
            dma((STEPS, slots)),
            dma((STEPS, slots)),
            dma((STEPS,)),
            dma((STEPS,)),
            dma((STEPS,)),
            dma((STEPS,)),
            dma((STEPS,)),
            dma((STEPS,)),
            dma((slots,)),
            dma((slots,)),
            dma((STEPS - 1, slots)),
            dma((STEPS - 1, slots)),
            pltpu.SemaphoreType.REGULAR((max(1, nz - 1), 2)),
        ],
        compiler_params=pltpu.CompilerParams(
            collective_id=0, has_side_effects=True, vmem_limit_bytes=62720 * 1024
        ),
    )(
        residual_in[0, 0],
        neumann[0, 0],
        dirichlet[0, 0],
        coarse[0],
        decay[0],
        face_rows[0],
        primal[0],
    )
    rows = unknowns // 2
    tall = pl.BlockSpec((rows, width), lambda i: (i, 0))
    sol, res = pl.pallas_call(
        closing,
        grid=(unknowns // rows,),
        out_shape=(whole, whole),
        in_specs=[inside] * 4,
        out_specs=(tall, tall),
        compiler_params=pltpu.CompilerParams(vmem_limit_bytes=16000 * 1024),
    )(*pieces)
    return (sol[None, None], res[None, None])


def solution(mesh):
    return jax.shard_map(
        functools.partial(local, mesh.shape["gx"], mesh.shape["gy"]),
        mesh=mesh,
        in_specs=(
            P("gx", "gy", None, None),
            P("gx", "gy", None, None),
            P("gx", "gy", None, None),
            P("gx", "gy", None),
            P("gx", "gy", None),
            P("gx", "gy", None),
            P("gx", "gy", None),
        ),
        out_specs=(P("gx", "gy", None, None), P("gx", "gy", None, None)),
        check_vma=False,
    )
```

```python
import functools

import jax
import jax.numpy as jnp
from jax import lax
from jax.experimental import pallas as pl
from jax.experimental.pallas import tpu as pltpu
from jax.sharding import PartitionSpec as P

STEPS = 2
CUTS = (0, 4, 8, 8)
UP_CUTS = (0, 2, 8, 8)
DOWN_CUTS = (0, 4, 8, 8)
MESH = pl.DeviceIdType.MESH
F32 = jnp.float32
BF16 = jnp.bfloat16


def dot(a, b):
    return jnp.dot(a, b, preferred_element_type=F32)


def split(x):
    high = x.astype(BF16)
    return high, (x - high.astype(F32)).astype(BF16)


def dot3(a, b):
    return dot(a[0], b[0]) + dot(a[0], b[1]) + dot(a[1], b[0])


def stacked3(a, b):
    rows = a.shape[0] // 2
    first = dot(a, b[0])
    return first[:rows] + first[rows:] + dot(a[:rows], b[1])


def tall3(x):
    high, low = split(x)
    return jnp.concatenate([high, low, high], axis=0)


def when(cond, body):
    if cond is True:
        body()
    elif cond is not False:
        pl.when(cond)(body)


def both(p, q):
    if p is True or q is False:
        return q
    if q is True or p is False:
        return p
    return jnp.logical_and(p, q)


def negate(p):
    return not p if isinstance(p, bool) else jnp.logical_not(p)


def line_sizes(count):
    chips = count // 2
    inner = 1
    while inner * inner * 4 <= chips:
        inner *= 2
    return chips // inner, inner


def x_slots(nx):
    return 1 if nx == 2 else 2


def kernel(
    nx, ny_all, r_hbm, n_hbm, d_hbm, c_hbm, decay_hbm, rows_hbm, prim_hbm,
    t1_ref, t2_ref, thin_ref, last_ref,
    n_buf, d_buf, nh, nl, dh, dl, perm, perm_t,
    r_buf, jump, high_v, low_v, high_w, low_w, fsend, frecv, fix, c_all, cs, psend, gath, qsend, cown, cprev, csend,
    sel, npp, base, decay_v, rows_v, prim_v, esend, erecv, edges, couple, chain_v, hsend, hrecv, cup, rate_out, rate_in,
    load_sem, small_sem, cf_ssem, cp_ssem, c_rsem, f_ssem, f_rsem, a_ssem, g_rsem,
    q_ssem, q_rsem, p_ssem, p_rsem, e_ssem, e_rsem, h_ssem, h_rsem, u_ssem, u_rsem, rate_sem, line_sem,
):
    unknowns, width = r_buf.shape
    face = unknowns // 4
    prims = c_all.shape[1]
    nz, ny = line_sizes(ny_all)
    ng = 2 * ny
    part = width // ng
    fold = max(1, 128 // part)
    short = prims // fold
    block = 2 * face
    blocks = unknowns // block
    xs = x_slots(nx)
    slots = xs + 2

    a = lax.axis_index("gx")
    me = lax.axis_index("gy")
    plane = 2 * ny
    core = me % 2
    y = me // 2 % ny
    z = me // plane
    partner = me + 1 - 2 * core

    team = z // ny * ny + y
    g = z % ny * 2 + core

    def member(which, j):
        return ((which // ny * ny + j // 2) * ny + which % ny) * 2 + j % 2

    smalls = [
        pltpu.make_async_copy(src, dst, small_sem.at[i])
        for i, (src, dst) in enumerate(
            [(rows_hbm, rows_v), (prim_hbm, prim_v), (decay_hbm, decay_v)]
        )
    ]
    loads = [
        pltpu.make_async_copy(src, dst, load_sem.at[i])
        for i, (src, dst) in enumerate(
            [(r_hbm, r_buf), (c_hbm, c_all.at[g]), (n_hbm, n_buf), (d_hbm, d_buf)]
        )
    ]
    smalls[0].start()
    loads[0].start()
    smalls[1].start()
    smalls[2].start()

    barrier = pltpu.get_barrier_semaphore()

    def greet(gx, gy):
        pl.semaphore_signal(barrier, inc=1, device_id=(gx, gy), device_id_type=MESH)

    out_slot = xs + core
    in_slot = xs + 1 - core
    outward = me - 1 + 2 * core
    has_out = jnp.logical_and(outward >= 0, outward < ny_all)
    links = [(has_out, (a, outward), out_slot, in_slot, None)]
    if nx == 2:
        links.append((True, (1 - a, me), 0, 0, a == 0))
    else:
        links.append((a > 0, (a - 1, me), 0, 1, False))
        links.append((a < nx - 1, (a + 1, me), 1, 0, True))
    links.append((True, (a, partner), in_slot, out_slot, None))
    mate_at = [
        (z + dz) % ny * 2 + (core + dc) % 2
        for dz, dc in [(0, 0)] + [(k, c) for k in range(1, ny) for c in range(2)] + [(0, 1)]
    ]
    mates = [member(team, j) for j in mate_at]
    below, above = z > 0, z < nz - 1
    count = jnp.int32(ng - 1 + plane - 1)
    for has, where, _, _, _ in links[:-1]:
        when(has, functools.partial(greet, *where))
        count = count + (1 if has is True else has.astype(jnp.int32))
    for d in range(1, ng):
        greet(a, mates[d])
    for d in range(1, plane):
        greet(a, z * plane + (me + d) % plane)
    pl.when(below)(functools.partial(greet, a, me - plane))
    pl.when(above)(functools.partial(greet, a, me + plane))
    count = count + below.astype(jnp.int32) + above.astype(jnp.int32)
    for has, there in ((a > 0, a - 1), (a < nx - 1, a + 1)):
        if nx > 1:

            @pl.when(has)
            def _(there=there):
                for d in range(1, ng):
                    greet(there, mates[d])

            count = count + has.astype(jnp.int32) * (ng - 1)

    def line_round(turn):
        def tell(low):
            pl.semaphore_signal(
                line_sem.at[turn, 1 if low else 0],
                inc=1,
                device_id=(a, me - plane if low else me + plane),
                device_id_type=MESH,
            )

        pl.when(below)(functools.partial(tell, True))
        pl.when(above)(functools.partial(tell, False))

    def line_wait(turn):
        pl.when(below)(lambda: pl.semaphore_wait(line_sem.at[turn, 0], 1))
        pl.when(above)(lambda: pl.semaphore_wait(line_sem.at[turn, 1], 1))

    turns = [0]

    def advance():
        turn = turns[0]
        if turn < nz - 1:
            line_wait(turn)
            if turn + 1 < nz - 1:
                line_round(turn + 1)
            turns[0] = turn + 1

    def pack(x, pieces=fold):
        size = x.shape[0] // pieces
        return jnp.concatenate([x[j * size : (j + 1) * size] for j in range(pieces)], axis=1)

    def unpack(x, columns=part):
        return jnp.concatenate(
            [x[:, j * columns : (j + 1) * columns] for j in range(x.shape[1] // columns)], axis=0
        )

    apart = pl.when(a >= 0)

    def rows_of(i, size):
        if isinstance(i, int):
            return pl.ds(i * size, size)
        return pl.ds(pl.multiple_of(i * size, size), size)

    def remote(src, dst, send, recv, gx, gy):
        return pltpu.make_async_remote_copy(
            src_ref=src, dst_ref=dst, send_sem=send, recv_sem=recv,
            device_id=(gx, gy), device_id_type=MESH,
        )

    def face_copy(step, link):
        _, where, here, there, _ = link
        return remote(
            fsend.at[step, rows_of(here, face), :],
            frecv.at[step, rows_of(there, face), :],
            f_ssem.at[step, here],
            f_rsem.at[step, there],
            *where,
        )

    def face_part(step, link, first, stop):
        _, where, here, there, _ = link
        size = face // 8

        def part_of(slot):
            start = slot * face + first * size
            if not isinstance(slot, int):
                start = pl.multiple_of(start, size)
            return pl.ds(start, (stop - first) * size)

        return remote(
            fsend.at[step, part_of(here), :],
            frecv.at[step, part_of(there), :],
            f_ssem.at[step, here],
            f_rsem.at[step, there],
            *where,
        )

    def send_part(step, stage, some):
        for link in some:
            for up, cuts in ((None, CUTS), (True, UP_CUTS), (False, DOWN_CUTS)):
                first, stop = cuts[stage], cuts[stage + 1]
                if first == stop or (up is None) != (link[4] is None):
                    continue
                side = True if up is None else link[4] if up else negate(link[4])
                when(both(link[0], side), face_part(step, link, first, stop).start)

    def edge_copy(link):
        _, where, here, there, _ = link
        return remote(
            esend.at[here], erecv.at[there], e_ssem.at[here], e_rsem.at[there], *where
        )

    def chain_copy(step, link):
        _, where, here, there, _ = link
        return remote(
            hsend.at[step], hrecv.at[step, there], h_ssem.at[step, here], h_rsem.at[step, there],
            *where,
        )

    def arrives(copy, link, cond=True):
        has, where, here, _, up = link
        when(both(has, cond), copy((has, where, here, here, up)).wait_recv)

    lanes = 128

    def face_lines(slot):
        if nx == 2:
            number = 1 - a if isinstance(slot, int) and slot == 0 else slot + 1
        else:
            number = slot
        return rows_v[:, rows_of(number, face)].astype(F32)

    def build_face(slot):
        column = jnp.transpose(jnp.broadcast_to(face_lines(slot), (lanes, face)))
        for t in range(unknowns // lanes):
            cols = lax.broadcasted_iota(jnp.int32, (face, lanes), 1) + t * lanes
            perm[rows_of(slot, face), t * lanes : (t + 1) * lanes] = jnp.where(
                column == cols.astype(F32), 1.0, 0.0
            ).astype(BF16)

    def take_faces(step, field, some):
        for link in some:

            @apart
            def _(at=rows_of(link[2], face)):
                picks = perm[at, :]
                fsend[step, at, :] = dot(picks, field[0]) + dot(picks, field[1])

    smalls[0].wait()
    for slot in range(slots):
        build_face(slot)
    loads[0].wait()
    for load in loads[1:]:
        load.start()
    field = split(r_buf[...])
    take_faces(0, field, links[:1])
    pl.semaphore_wait(barrier, count)
    when(links[0][0], face_copy(0, links[0]).start)
    for link in links[1:]:
        take_faces(0, field, [link])
        when(link[0], face_copy(0, link).start)
    if nz > 1:
        line_round(0)

    along = [(z + dy) % ny for dy in range(ny)]

    def coarse_far(dy):
        return remote(
            c_all.at[g], c_all.at[g], cf_ssem.at[dy], c_rsem.at[g],
            a, member(team, along[dy] * 2 + core),
        )

    def coarse_near(dy):
        which = along[dy] * 2 + core
        return remote(
            c_all.at[which], c_all.at[which], cp_ssem.at[dy], c_rsem.at[which], a, partner
        )

    def coarse_arrived(which):
        remote(
            c_all.at[which], c_all.at[which], cp_ssem.at[0], c_rsem.at[which], a, partner
        ).wait_recv()

    loads[1].wait()
    coarse_near(0).start()
    for dy in range(1, ny):
        coarse_far(dy).start()

    for link in links[:-1]:
        if link[0] is not True:

            @pl.when(jnp.logical_not(link[0]))
            def _(link=link):
                here = link[2]
                for step in range(STEPS):
                    frecv[step, rows_of(here, face), :] = jnp.zeros((face, width), F32)
                erecv[here] = jnp.zeros(erecv.shape[1:], F32)
                for step in range(STEPS - 1):
                    hrecv[step, here] = jnp.zeros((prims, width), F32)

    lines = jnp.concatenate([face_lines(slot) for slot in range(slots)], axis=1)

    def build_t(i, carry):
        at = rows_of(i, block)
        here = lax.broadcasted_iota(jnp.int32, (block, slots * face), 0) + i * block
        perm_t[at, :] = jnp.where(here.astype(F32) == lines, 1.0, 0.0).astype(BF16)
        return carry

    lax.fori_loop(0, blocks, build_t, 0)

    smalls[1].wait()
    smalls[2].wait()
    eye = lax.broadcasted_iota(jnp.int32, (prims, prims), 0) == lax.broadcasted_iota(
        jnp.int32, (prims, prims), 1
    )
    prim_row = prim_v[...].astype(F32)
    prim_col = jnp.sum(jnp.where(eye, prim_row, 0.0), axis=1, keepdims=True)
    rate_out[...] = jnp.broadcast_to(
        jnp.concatenate([decay_v[...]] * (128 // prims), axis=1), rate_out.shape
    )

    def rate_copy():
        return remote(rate_out, rate_in, rate_sem.at[0], rate_sem.at[1], a - 1, me)

    if nx > 1:
        pl.when(a > 0)(rate_copy().start)
    rate = jnp.sum(jnp.where(eye, decay_v[...], 0.0), axis=1, keepdims=True)
    pick_t = jnp.where(
        prim_col == lax.broadcasted_iota(jnp.int32, (prims, unknowns), 1).astype(F32), 1.0, 0.0
    ).astype(BF16)
    thrice = jnp.concatenate([prim_row] * 3, axis=1)
    tops = lax.broadcasted_iota(jnp.int32, (unknowns, 3 * prims), 0).astype(F32) == thrice
    high_side = lax.broadcasted_iota(jnp.int32, (unknowns, 3 * prims), 1) < 2 * prims
    pick_h = jnp.where(jnp.logical_and(tops, high_side), 1.0, 0.0).astype(BF16)
    pick_l = jnp.where(
        jnp.logical_and(tops, jnp.logical_not(high_side)), 1.0, 0.0
    ).astype(BF16)
    loads[2].wait()

    def halve(i, carry):
        at = rows_of(i, block)
        nh[at, :], nl[at, :] = split(n_buf[at, :])
        return carry

    lax.fori_loop(0, blocks, halve, 0)
    advance()
    sel[0:prims, :] = dot(pick_t, nh[...]).astype(BF16)
    sel[prims : 2 * prims, :] = dot(pick_t, nl[...]).astype(BF16)
    advance()
    npp[...] = dot(sel[...], perm_t[...]).astype(BF16)
    base[...] = stacked3(sel[...], field)
    advance()
    loads[3].wait()

    def halve_pick(i, carry):
        at = rows_of(i, block)
        high, low = split(d_buf[at, :])
        dh[at, :] = high
        dl[at, :] = low
        thin_ref[at, :] = (dot(high, pick_h) + dot(low, pick_l)).astype(BF16)
        return carry

    lax.fori_loop(0, blocks, halve_pick, 0)
    for _ in range(nz):
        advance()
    lifted = dot(perm[...], thin_ref[...])
    lifted = lifted[:, :prims] + lifted[:, 2 * prims :]
    for slot in range(slots):
        esend[slot] = pack(lifted[slot * face : (slot + 1) * face], 128 // prims)
    for link in links:
        when(link[0], edge_copy(link).start)

    order = [
        (dz, d)
        for dz in sorted(range(nz), key=lambda dz: -min(dz, nz - dz))
        for d in range(ng)
        if (dz, d) != (0, 0)
    ]

    def spread(step, dz, d):
        return remote(
            psend.at[step, mate_at[d]],
            gath.at[step, me],
            a_ssem.at[step],
            g_rsem.at[step],
            a,
            member((team + dz) % nz, mate_at[d]),
        )

    def all_spread(step):
        every = gath.at[step, pl.ds(0, ny_all - 1)]
        return remote(every, every, a_ssem.at[step], g_rsem.at[step], a, partner)

    def q_copy(step, d):
        return remote(
            qsend.at[step, mate_at[d]], cown.at[step, g], q_ssem.at[step], q_rsem.at[step],
            a, mates[d],
        )

    def first_copy(step, d):
        return remote(
            qsend.at[step, mate_at[d]], cprev.at[step, g], p_ssem.at[step], p_rsem.at[step],
            a + 1, mates[d],
        )

    def next_copy(step, q):
        return remote(
            csend.at[step, q], cprev.at[step, q], p_ssem.at[step], p_rsem.at[step],
            a + 1, me,
        )

    def all_q(step):
        every = cown.at[step, pl.ds(0, ng - 1)]
        return remote(every, every, q_ssem.at[step], q_rsem.at[step], a, partner)

    def down_copy(step, d):
        return remote(
            qsend.at[step, mate_at[d]], cup.at[step, g], u_ssem.at[step], u_rsem.at[step],
            a - 1, mates[d],
        )

    def all_u(step):
        every = cup.at[step]
        return remote(every, every, u_ssem.at[step], u_rsem.at[step], a, partner)

    def all_p(step):
        every = cprev.at[step]
        return remote(every, every, p_ssem.at[step], p_rsem.at[step], a, partner)

    starts = jnp.logical_and(a == 0, a < nx - 1)
    passes = jnp.logical_and(a > 0, a < nx - 1)

    def sent_later(step):
        if step == 0:
            if nx > 1:
                pl.when(a > 0)(rate_copy().wait_send)
            coarse_near(0).wait_send()
            for dy in range(1, ny):
                coarse_far(dy).wait_send()
                coarse_near(dy).wait_send()
            for link in links:
                when(link[0], edge_copy(link).wait_send)
                when(link[0], face_copy(0, link).wait_send)
        if step + 1 < STEPS:
            for link in links:
                when(link[0], face_copy(step + 1, link).wait_send)
                if link[4] is None:
                    when(link[0], chain_copy(step, link).wait_send)
            if nx > 1:
                pl.when(a > 0)(all_u(step).wait_send)
        all_q(step).wait_send()
        pl.when(a < nx - 1)(all_p(step).wait_send)

    for step in range(STEPS):
        last = step + 1 == STEPS
        if step == 0:
            arrives(functools.partial(face_copy, step), links[-1])
            inner = pl.ds(pl.multiple_of(in_slot * face, face), face)
            ghost = split(frecv[step, inner, :])

            def start_fill(i, carry, ghost=ghost, inner=inner):
                at = rows_of(i, block)
                back = perm_t[at, inner]
                jump[at, :] = r_buf[at, :] - dot(back, ghost[0]) - dot(back, ghost[1])
                return carry

            lax.fori_loop(0, blocks, start_fill, 0)
            for link in links[:-1]:
                arrives(functools.partial(face_copy, step), link)

            @apart
            def _(step=step):
                base[...] -= stacked3(npp[...], split(frecv[step]))

            prim = base[...]
        else:
            for link in links:
                arrives(functools.partial(face_copy, step), link)

            @apart
            def _(step=step):
                base[...] -= stacked3(npp[...], split(frecv[step]))

            for link in links:
                if link[4] is None:
                    arrives(functools.partial(chain_copy, step - 1), link)
            beside = jnp.concatenate([tall3(hrecv[step - 1, slot]) for slot in range(slots)])
            prim = base[...] + dot(couple[...], beside)
        for q in range(ng):
            psend[step, q] = pack(prim[:, q * part : (q + 1) * part])
        for dz, d in order:
            spread(step, dz, d).start()
        gath[step, me] = psend[step, g]
        if step == 0:
            outer = pl.ds(pl.multiple_of(out_slot * face, face), face)
            sides = [(pl.ds(slot * face, face)) for slot in range(xs)] + [outer]
            ghosts = [split(frecv[step, side, :]) for side in sides]
        else:
            for slot in range(slots):
                at = slice(slot * face, (slot + 1) * face)
                fix[at, :] = frecv[step, at, :] - 0.5 * dot(
                    edges[at, :], beside[slot * 3 * prims : (slot + 1) * 3 * prims]
                )
            sides = [pl.ds(0, slots * face)]
            ghosts = [split(fix[...])]

        def fill(i, carry, step=step, sides=sides, ghosts=ghosts):
            at = rows_of(i, block)
            value = jump[at, :] if step == 0 else t2_ref[at, :]
            for side, ghost in zip(sides, ghosts):
                back = perm_t[at, side]
                value = value - dot(back, ghost[0]) - dot(back, ghost[1])
            jump[at, :] = value
            high_v[at, :], low_v[at, :] = split(value)
            return carry

        lax.fori_loop(0, blocks, fill, 0)

        def multiply(i, carry):
            at = rows_of(i, block)
            work = dot3((nh[at, :], nl[at, :]), (high_v[...], low_v[...]))
            high_w[at, :], low_w[at, :] = split(work)
            return carry

        lax.fori_loop(0, blocks, multiply, 0)
        if step == 0:
            for dy in range(1, ny):
                coarse_arrived(along[dy] * 2 + core)
                coarse_near(dy).start()

        def smooth(i, carry, step=step, last=last):
            at = rows_of(i, block)
            update = dot3((dh[at, :], dl[at, :]), (high_w[...], low_w[...]))
            if step == 0:
                t1_ref[at, :] = update
            else:
                t1_ref[at, :] += update
            rest = jump[at, :] - 0.5 * update
            t2_ref[at, :] = rest
            if not last:
                high_v[at, :], low_v[at, :] = split(rest)
            return carry

        lax.fori_loop(0, blocks, smooth, 0)
        if not last:
            rests = (high_v[...], low_v[...])
            for link in links[:-1]:
                take_faces(step + 1, rests, [link])
                send_part(step + 1, 0, [link])
            take_faces(step + 1, rests, links[-1:])
            face_copy(step + 1, links[-1]).start()
        if step == 0:
            for dy in range(ny):
                coarse_arrived(along[dy] * 2 + 1 - core)
            size = ng * prims
            cs[0:size, :], cs[size : 2 * size, :] = split(
                c_all[...].reshape(size, c_all.shape[2])
            )
        if step > 0:
            sent_later(step - 1)
        all_spread(step).wait_recv()

        @apart
        def _(step=step):
            values = jnp.concatenate([unpack(gath[step, b]) for b in range(ny_all)], axis=0)
            quarter = stacked3(cs[...], split(values))
            for q in range(ng):
                qsend[step, q] = pack(quarter[q * prims : (q + 1) * prims, :])

        @pl.when(starts)
        def _(step=step):
            for d in [*range(1, ng), 0]:
                first_copy(step, d).start()

        for d in range(1, ng):
            q_copy(step, d).start()
        if nx > 1 and not last:

            @pl.when(a > 0)
            def _(step=step):
                for d in [*range(1, ng), 0]:
                    down_copy(step, d).start()

        if not last:
            send_part(step + 1, 1, links[:-1])
        cown[step, g] = qsend[step, g]
        all_spread(step).wait_send()
        all_q(step).wait_recv()

        def joined(ref, step=step):
            return jnp.concatenate([unpack(ref[step, q]) for q in range(ng)], axis=1)

        chain_out = last_ref if last else hsend.at[step]

        @pl.when(a == 0)
        def _(chain_out=chain_out):
            chain_out[...] = joined(cown)

        @pl.when(a > 0)
        def _(step=step, chain_out=chain_out):
            chain_v[...] = joined(cown)
            all_p(step).wait_recv()
            chain_out[...] = chain_v[...] + rate * joined(cprev)

        @pl.when(passes)
        def _(step=step, chain_out=chain_out):
            for q in range(ng):
                csend[step, q] = pack(chain_out[:, q * part : (q + 1) * part])
                next_copy(step, q).start()

        if not last:
            for link in links:
                if link[4] is None:
                    when(link[0], chain_copy(step, link).start)
            send_part(step + 1, 2, links[:-1])
            chain = tall3(hsend[step])

            def finish(i, carry, chain=chain):
                at = rows_of(i, block)
                more = dot(thin_ref[at, :], chain)
                t1_ref[at, :] += more
                t2_ref[at, :] -= 0.5 * more
                return carry

            lax.fori_loop(0, blocks, finish, 0)
            base[...] = stacked3(sel[...], split(t2_ref[...]))
            if nx > 1:

                @pl.when(a > 0)
                def _(step=step):
                    hrecv[step, 0] = joined(cprev)

                @pl.when(a < nx - 1)
                def _(step=step):
                    if step == 0:
                        rate_copy().wait_recv()
                    all_u(step).wait_recv()
                    above_row = rate_in[0:1, :prims]
                    rate_up = jnp.sum(jnp.where(eye, above_row, 0.0), axis=1, keepdims=True)
                    hrecv[step, xs - 1] = joined(cup) + rate_up * hsend[step]
            if step == 0:
                for link in links:
                    arrives(edge_copy, link)
                for slot in range(slots):
                    at = slice(slot * face, (slot + 1) * face)
                    high, low = split(unpack(erecv[slot], prims))
                    edges[at, :] = jnp.concatenate([high, high, low], axis=1)
                    both_ways = dot(npp[:, at], edges[at, :])
                    across = both_ways[:prims, :prims] + both_ways[:prims, 2 * prims :]
                    high, low = split(0.5 * (across + both_ways[prims:, :prims]))
                    for k, piece_of in enumerate((high, high, low)):
                        left = (3 * slot + k) * prims
                        couple[:, left : left + prims] = piece_of
    sent_later(STEPS - 1)


def closing(t1, t2, thin, chain, sol, res):
    rows = sol.shape[0]
    at = pl.ds(pl.multiple_of(pl.program_id(0) * rows, rows), rows)
    more = dot(thin[at, :], tall3(chain[...]))
    sol[...] = t1[at, :] + more
    res[...] = t2[at, :] - 0.5 * more


def local(nx, ny_all, residual_in, neumann, dirichlet, coarse, decay, face_rows, primal):
    unknowns, width = residual_in.shape[2:]
    prims = primal.shape[2]
    order = coarse.shape[2]
    nz, ny = line_sizes(ny_all)
    ng = 2 * ny
    part = width // ng
    fold = max(1, 128 // part)
    piece = (prims // fold, fold * part)
    face = unknowns // 4
    slots = x_slots(nx) + 2
    anywhere = pl.BlockSpec(memory_space=pl.ANY)
    inside = pl.BlockSpec(memory_space=pltpu.VMEM)
    square = (unknowns, unknowns)
    field = (unknowns, width)
    ghosts = (slots * face, width)
    edge = (slots, face * prims // 128, 128)
    dma = pltpu.SemaphoreType.DMA
    whole = jax.ShapeDtypeStruct(field, F32)
    outs = [(field, F32), (field, F32), ((unknowns, 3 * prims), BF16), ((prims, width), F32)]
    pieces = pl.pallas_call(
        functools.partial(kernel, nx, ny_all),
        out_shape=tuple(pltpu.VMEM(shape, kind) for shape, kind in outs),
        in_specs=[anywhere] * 7,
        out_specs=(inside,) * 4,
        scratch_shapes=[
            pltpu.VMEM(square, F32),
            pltpu.VMEM(square, F32),
        ]
        + [pltpu.VMEM(square, BF16)] * 4
        + [
            pltpu.VMEM((slots * face, unknowns), BF16),
            pltpu.VMEM((unknowns, slots * face), BF16),
        ]
        + [pltpu.VMEM(field, F32)] * 2
        + [pltpu.VMEM(field, BF16)] * 4
        + [
            pltpu.VMEM((STEPS,) + ghosts, F32),
            pltpu.VMEM((STEPS,) + ghosts, F32),
            pltpu.VMEM(ghosts, F32),
            pltpu.VMEM((ng, prims, order), F32),
            pltpu.VMEM((2 * ng * prims, order), BF16),
            pltpu.VMEM((STEPS, ng) + piece, F32),
            pltpu.VMEM((STEPS, ny_all) + piece, F32),
            pltpu.VMEM((STEPS, ng) + piece, F32),
            pltpu.VMEM((STEPS, ng) + piece, F32),
            pltpu.VMEM((STEPS, ng) + piece, F32),
            pltpu.VMEM((STEPS, ng) + piece, F32),
            pltpu.VMEM((2 * prims, unknowns), BF16),
            pltpu.VMEM((2 * prims, slots * face), BF16),
            pltpu.VMEM((prims, width), F32),
            pltpu.VMEM((1, prims), F32),
            pltpu.VMEM((1, unknowns), jnp.int32),
            pltpu.VMEM((1, prims), jnp.int32),
            pltpu.VMEM(edge, F32),
            pltpu.VMEM(edge, F32),
            pltpu.VMEM((slots * face, 3 * prims), BF16),
            pltpu.VMEM((prims, slots * 3 * prims), BF16),
            pltpu.VMEM((prims, width), F32),
            pltpu.VMEM((STEPS - 1, prims, width), F32),
            pltpu.VMEM((STEPS - 1, slots, prims, width), F32),
            pltpu.VMEM((STEPS - 1, ng) + piece, F32),
            pltpu.VMEM((8, 128), F32),
            pltpu.VMEM((8, 128), F32),
            dma((4,)),
            dma((3,)),
            dma((ny,)),
            dma((ny,)),
            dma((ng,)),
            dma((STEPS, slots)),
            dma((STEPS, slots)),
            dma((STEPS,)),
            dma((STEPS,)),
            dma((STEPS,)),
            dma((STEPS,)),
            dma((STEPS,)),
            dma((STEPS,)),
            dma((slots,)),
            dma((slots,)),
            dma((STEPS - 1, slots)),
            dma((STEPS - 1, slots)),
            dma((STEPS - 1,)),
            dma((STEPS - 1,)),
            dma((2,)),
            pltpu.SemaphoreType.REGULAR((max(1, nz - 1), 2)),
        ],
        compiler_params=pltpu.CompilerParams(
            collective_id=0, has_side_effects=True, vmem_limit_bytes=62720 * 1024
        ),
    )(
        residual_in[0, 0],
        neumann[0, 0],
        dirichlet[0, 0],
        coarse[0],
        decay[0],
        face_rows[0],
        primal[0],
    )
    rows = unknowns // 2
    tall = pl.BlockSpec((rows, width), lambda i: (i, 0))
    sol, res = pl.pallas_call(
        closing,
        grid=(unknowns // rows,),
        out_shape=(whole, whole),
        in_specs=[inside] * 4,
        out_specs=(tall, tall),
        compiler_params=pltpu.CompilerParams(vmem_limit_bytes=16000 * 1024),
    )(*pieces)
    return (sol[None, None], res[None, None])


def solution(mesh):
    return jax.shard_map(
        functools.partial(local, mesh.shape["gx"], mesh.shape["gy"]),
        mesh=mesh,
        in_specs=(
            P("gx", "gy", None, None),
            P("gx", "gy", None, None),
            P("gx", "gy", None, None),
            P("gx", "gy", None),
            P("gx", "gy", None),
            P("gx", "gy", None),
            P("gx", "gy", None),
        ),
        out_specs=(P("gx", "gy", None, None), P("gx", "gy", None, None)),
        check_vma=False,
    )
```

```python
import functools

import jax
import jax.numpy as jnp
from jax import lax
from jax.experimental import pallas as pl
from jax.experimental.pallas import tpu as pltpu
from jax.sharding import PartitionSpec as P

STEPS = 2
CUTS = (0, 4, 8, 8)
UP_CUTS = (0, 2, 8, 8)
DOWN_CUTS = (0, 4, 8, 8)
MESH = pl.DeviceIdType.MESH
F32 = jnp.float32
BF16 = jnp.bfloat16


def dot(a, b):
    return jnp.dot(a, b, preferred_element_type=F32)


def split(x):
    high = x.astype(BF16)
    return high, (x - high.astype(F32)).astype(BF16)


def dot3(a, b):
    return dot(a[0], b[0]) + dot(a[0], b[1]) + dot(a[1], b[0])


def stacked3(a, b):
    rows = a.shape[0] // 2
    first = dot(a, b[0])
    return first[:rows] + first[rows:] + dot(a[:rows], b[1])


def tall3(x):
    high, low = split(x)
    return jnp.concatenate([high, low, high], axis=0)


def when(cond, body):
    if cond is True:
        body()
    elif cond is not False:
        pl.when(cond)(body)


def both(p, q):
    if p is True or q is False:
        return q
    if q is True or p is False:
        return p
    return jnp.logical_and(p, q)


def negate(p):
    return not p if isinstance(p, bool) else jnp.logical_not(p)


def line_sizes(count):
    chips = count // 2
    inner = 1
    while inner * inner * 4 <= chips:
        inner *= 2
    return chips // inner, inner


def x_slots(nx):
    return 1 if nx == 2 else 2


def kernel(
    nx, ny_all, r_hbm, n_hbm, d_hbm, c_hbm, decay_hbm, rows_hbm, prim_hbm,
    t1_ref, t2_ref, thin_ref, last_ref,
    n_buf, d_buf, nh, nl, dh, dl, perm, perm_t,
    r_buf, jump, high_v, low_v, high_w, low_w, fsend, frecv, fix, c_all, cs, psend, gath, qsend, cown, cprev, csend,
    sel, npp, base, decay_v, rows_v, prim_v, esend, erecv, edges, couple, chain_v, hsend, hrecv, cup, rate_out, rate_in,
    load_sem, small_sem, cf_ssem, cp_ssem, c_rsem, f_ssem, f_rsem, a_ssem, g_rsem,
    q_ssem, q_rsem, p_ssem, p_rsem, e_ssem, e_rsem, h_ssem, h_rsem, u_ssem, u_rsem, rate_sem, line_sem,
):
    unknowns, width = r_buf.shape
    face = unknowns // 4
    prims = c_all.shape[1]
    nz, ny = line_sizes(ny_all)
    ng = 2 * ny
    part = width // ng
    fold = max(1, 128 // part)
    short = prims // fold
    block = 2 * face
    blocks = unknowns // block
    xs = x_slots(nx)
    slots = xs + 2

    a = lax.axis_index("gx")
    me = lax.axis_index("gy")
    plane = 2 * ny
    core = me % 2
    y = me // 2 % ny
    z = me // plane
    partner = me + 1 - 2 * core

    team = z // ny * ny + y
    g = z % ny * 2 + core

    def member(which, j):
        return ((which // ny * ny + j // 2) * ny + which % ny) * 2 + j % 2

    smalls = [
        pltpu.make_async_copy(src, dst, small_sem.at[i])
        for i, (src, dst) in enumerate(
            [(rows_hbm, rows_v), (prim_hbm, prim_v), (decay_hbm, decay_v)]
        )
    ]
    loads = [
        pltpu.make_async_copy(src, dst, load_sem.at[i])
        for i, (src, dst) in enumerate(
            [(r_hbm, r_buf), (c_hbm, c_all.at[g]), (n_hbm, n_buf), (d_hbm, d_buf)]
        )
    ]
    smalls[0].start()
    loads[0].start()
    smalls[1].start()
    smalls[2].start()

    barrier = pltpu.get_barrier_semaphore()

    def greet(gx, gy):
        pl.semaphore_signal(barrier, inc=1, device_id=(gx, gy), device_id_type=MESH)

    out_slot = xs + core
    in_slot = xs + 1 - core
    outward = me - 1 + 2 * core
    has_out = jnp.logical_and(outward >= 0, outward < ny_all)
    links = [(has_out, (a, outward), out_slot, in_slot, None)]
    if nx == 2:
        links.append((True, (1 - a, me), 0, 0, a == 0))
    else:
        links.append((a > 0, (a - 1, me), 0, 1, False))
        links.append((a < nx - 1, (a + 1, me), 1, 0, True))
    links.append((True, (a, partner), in_slot, out_slot, None))
    mate_at = [
        (z + dz) % ny * 2 + (core + dc) % 2
        for dz, dc in [(0, 0)] + [(k, c) for k in range(1, ny) for c in range(2)] + [(0, 1)]
    ]
    mates = [member(team, j) for j in mate_at]
    below, above = z > 0, z < nz - 1
    count = jnp.int32(ng - 1 + plane - 1)
    for has, where, _, _, _ in links[:-1]:
        when(has, functools.partial(greet, *where))
        count = count + (1 if has is True else has.astype(jnp.int32))
    for d in range(1, ng):
        greet(a, mates[d])
    for d in range(1, plane):
        greet(a, z * plane + (me + d) % plane)
    pl.when(below)(functools.partial(greet, a, me - plane))
    pl.when(above)(functools.partial(greet, a, me + plane))
    count = count + below.astype(jnp.int32) + above.astype(jnp.int32)
    for has, there in ((a > 0, a - 1), (a < nx - 1, a + 1)):
        if nx > 1:

            @pl.when(has)
            def _(there=there):
                for d in range(1, ng):
                    greet(there, mates[d])

            count = count + has.astype(jnp.int32) * (ng - 1)

    def line_round(turn):
        def tell(low):
            pl.semaphore_signal(
                line_sem.at[turn, 1 if low else 0],
                inc=1,
                device_id=(a, me - plane if low else me + plane),
                device_id_type=MESH,
            )

        pl.when(below)(functools.partial(tell, True))
        pl.when(above)(functools.partial(tell, False))

    def line_wait(turn):
        pl.when(below)(lambda: pl.semaphore_wait(line_sem.at[turn, 0], 1))
        pl.when(above)(lambda: pl.semaphore_wait(line_sem.at[turn, 1], 1))

    turns = [0]

    def advance():
        turn = turns[0]
        if turn < nz - 1:
            line_wait(turn)
            if turn + 1 < nz - 1:
                line_round(turn + 1)
            turns[0] = turn + 1

    def pack(x, pieces=fold):
        size = x.shape[0] // pieces
        return jnp.concatenate([x[j * size : (j + 1) * size] for j in range(pieces)], axis=1)

    def unpack(x, columns=part):
        return jnp.concatenate(
            [x[:, j * columns : (j + 1) * columns] for j in range(x.shape[1] // columns)], axis=0
        )

    apart = pl.when(a >= 0)

    def rows_of(i, size):
        if isinstance(i, int):
            return pl.ds(i * size, size)
        return pl.ds(pl.multiple_of(i * size, size), size)

    def remote(src, dst, send, recv, gx, gy):
        return pltpu.make_async_remote_copy(
            src_ref=src, dst_ref=dst, send_sem=send, recv_sem=recv,
            device_id=(gx, gy), device_id_type=MESH,
        )

    def face_copy(step, link):
        _, where, here, there, _ = link
        return remote(
            fsend.at[step, rows_of(here, face), :],
            frecv.at[step, rows_of(there, face), :],
            f_ssem.at[step, here],
            f_rsem.at[step, there],
            *where,
        )

    def face_part(step, link, first, stop):
        _, where, here, there, _ = link
        size = face // 8

        def part_of(slot):
            start = slot * face + first * size
            if not isinstance(slot, int):
                start = pl.multiple_of(start, size)
            return pl.ds(start, (stop - first) * size)

        return remote(
            fsend.at[step, part_of(here), :],
            frecv.at[step, part_of(there), :],
            f_ssem.at[step, here],
            f_rsem.at[step, there],
            *where,
        )

    def send_part(step, stage, some):
        for link in some:
            for up, cuts in ((None, CUTS), (True, UP_CUTS), (False, DOWN_CUTS)):
                first, stop = cuts[stage], cuts[stage + 1]
                if first == stop or (up is None) != (link[4] is None):
                    continue
                side = True if up is None else link[4] if up else negate(link[4])
                when(both(link[0], side), face_part(step, link, first, stop).start)

    def edge_copy(link):
        _, where, here, there, _ = link
        return remote(
            esend.at[here], erecv.at[there], e_ssem.at[here], e_rsem.at[there], *where
        )

    def chain_copy(step, link):
        _, where, here, there, _ = link
        return remote(
            hsend.at[step], hrecv.at[step, there], h_ssem.at[step, here], h_rsem.at[step, there],
            *where,
        )

    def arrives(copy, link, cond=True):
        has, where, here, _, up = link
        when(both(has, cond), copy((has, where, here, here, up)).wait_recv)

    lanes = 128

    def face_lines(slot):
        if nx == 2:
            number = 1 - a if isinstance(slot, int) and slot == 0 else slot + 1
        else:
            number = slot
        return rows_v[:, rows_of(number, face)].astype(F32)

    def build_face(slot):
        column = jnp.transpose(jnp.broadcast_to(face_lines(slot), (lanes, face)))
        for t in range(unknowns // lanes):
            cols = lax.broadcasted_iota(jnp.int32, (face, lanes), 1) + t * lanes
            perm[rows_of(slot, face), t * lanes : (t + 1) * lanes] = jnp.where(
                column == cols.astype(F32), 1.0, 0.0
            ).astype(BF16)

    def take_faces(step, field, some):
        for link in some:

            @apart
            def _(at=rows_of(link[2], face)):
                picks = perm[at, :]
                fsend[step, at, :] = dot(picks, field[0]) + dot(picks, field[1])

    smalls[0].wait()
    for slot in range(slots):
        build_face(slot)
    loads[0].wait()
    for load in loads[1:]:
        load.start()
    field = split(r_buf[...])
    take_faces(0, field, links[:1])
    pl.semaphore_wait(barrier, count)
    when(links[0][0], face_copy(0, links[0]).start)
    for link in links[1:]:
        take_faces(0, field, [link])
        when(link[0], face_copy(0, link).start)
    if nz > 1:
        line_round(0)

    along = [(z + dy) % ny for dy in range(ny)]

    def coarse_far(dy):
        return remote(
            c_all.at[g], c_all.at[g], cf_ssem.at[dy], c_rsem.at[g],
            a, member(team, along[dy] * 2 + core),
        )

    def coarse_near(dy):
        which = along[dy] * 2 + core
        return remote(
            c_all.at[which], c_all.at[which], cp_ssem.at[dy], c_rsem.at[which], a, partner
        )

    def coarse_arrived(which):
        remote(
            c_all.at[which], c_all.at[which], cp_ssem.at[0], c_rsem.at[which], a, partner
        ).wait_recv()

    loads[1].wait()
    coarse_near(0).start()
    for dy in range(1, ny):
        coarse_far(dy).start()

    for link in links[:-1]:
        if link[0] is not True:

            @pl.when(jnp.logical_not(link[0]))
            def _(link=link):
                here = link[2]
                for step in range(STEPS):
                    frecv[step, rows_of(here, face), :] = jnp.zeros((face, width), F32)
                erecv[here] = jnp.zeros(erecv.shape[1:], F32)
                for step in range(STEPS - 1):
                    hrecv[step, here] = jnp.zeros((prims, width), F32)

    lines = jnp.concatenate([face_lines(slot) for slot in range(slots)], axis=1)

    def build_t(i, carry):
        at = rows_of(i, block)
        here = lax.broadcasted_iota(jnp.int32, (block, slots * face), 0) + i * block
        perm_t[at, :] = jnp.where(here.astype(F32) == lines, 1.0, 0.0).astype(BF16)
        return carry

    lax.fori_loop(0, blocks, build_t, 0)

    smalls[1].wait()
    smalls[2].wait()
    eye = lax.broadcasted_iota(jnp.int32, (prims, prims), 0) == lax.broadcasted_iota(
        jnp.int32, (prims, prims), 1
    )
    prim_row = prim_v[...].astype(F32)
    prim_col = jnp.sum(jnp.where(eye, prim_row, 0.0), axis=1, keepdims=True)
    rate_out[...] = jnp.broadcast_to(
        jnp.concatenate([decay_v[...]] * (128 // prims), axis=1), rate_out.shape
    )

    def rate_copy():
        return remote(rate_out, rate_in, rate_sem.at[0], rate_sem.at[1], a - 1, me)

    if nx > 1:
        pl.when(a > 0)(rate_copy().start)
    rate = jnp.sum(jnp.where(eye, decay_v[...], 0.0), axis=1, keepdims=True)
    pick_t = jnp.where(
        prim_col == lax.broadcasted_iota(jnp.int32, (prims, unknowns), 1).astype(F32), 1.0, 0.0
    ).astype(BF16)
    thrice = jnp.concatenate([prim_row] * 3, axis=1)
    tops = lax.broadcasted_iota(jnp.int32, (unknowns, 3 * prims), 0).astype(F32) == thrice
    high_side = lax.broadcasted_iota(jnp.int32, (unknowns, 3 * prims), 1) < 2 * prims
    pick_h = jnp.where(jnp.logical_and(tops, high_side), 1.0, 0.0).astype(BF16)
    pick_l = jnp.where(
        jnp.logical_and(tops, jnp.logical_not(high_side)), 1.0, 0.0
    ).astype(BF16)
    loads[2].wait()

    def halve(i, carry):
        at = rows_of(i, block)
        nh[at, :], nl[at, :] = split(n_buf[at, :])
        return carry

    lax.fori_loop(0, blocks, halve, 0)
    advance()
    sel[0:prims, :] = dot(pick_t, nh[...]).astype(BF16)
    sel[prims : 2 * prims, :] = dot(pick_t, nl[...]).astype(BF16)
    advance()
    npp[...] = dot(sel[...], perm_t[...]).astype(BF16)
    base[...] = stacked3(sel[...], field)
    advance()
    loads[3].wait()

    def halve_pick(i, carry):
        at = rows_of(i, block)
        high, low = split(d_buf[at, :])
        dh[at, :] = high
        dl[at, :] = low
        thin_ref[at, :] = (dot(high, pick_h) + dot(low, pick_l)).astype(BF16)
        return carry

    lax.fori_loop(0, blocks, halve_pick, 0)
    for _ in range(nz):
        advance()
    lifted = dot(perm[...], thin_ref[...])
    lifted = lifted[:, :prims] + lifted[:, 2 * prims :]
    for slot in range(slots):
        esend[slot] = pack(lifted[slot * face : (slot + 1) * face], 128 // prims)
    for link in links:
        when(link[0], edge_copy(link).start)

    order = [
        (dz, d)
        for dz in sorted(range(nz), key=lambda dz: -min(dz, nz - dz))
        for d in range(ng)
        if (dz, d) != (0, 0)
    ]

    def spread(step, dz, d):
        return remote(
            psend.at[step, mate_at[d]],
            gath.at[step, me],
            a_ssem.at[step],
            g_rsem.at[step],
            a,
            member((team + dz) % nz, mate_at[d]),
        )

    def all_spread(step):
        every = gath.at[step, pl.ds(0, ny_all - 1)]
        return remote(every, every, a_ssem.at[step], g_rsem.at[step], a, partner)

    def q_copy(step, d):
        return remote(
            qsend.at[step, mate_at[d]], cown.at[step, g], q_ssem.at[step], q_rsem.at[step],
            a, mates[d],
        )

    def first_copy(step, d):
        return remote(
            qsend.at[step, mate_at[d]], cprev.at[step, g], p_ssem.at[step], p_rsem.at[step],
            a + 1, mates[d],
        )

    def next_copy(step, q):
        return remote(
            csend.at[step, q], cprev.at[step, q], p_ssem.at[step], p_rsem.at[step],
            a + 1, me,
        )

    def all_q(step):
        every = cown.at[step, pl.ds(0, ng - 1)]
        return remote(every, every, q_ssem.at[step], q_rsem.at[step], a, partner)

    def down_copy(step, d):
        return remote(
            qsend.at[step, mate_at[d]], cup.at[step, g], u_ssem.at[step], u_rsem.at[step],
            a - 1, mates[d],
        )

    def all_u(step):
        every = cup.at[step]
        return remote(every, every, u_ssem.at[step], u_rsem.at[step], a, partner)

    def all_p(step):
        every = cprev.at[step]
        return remote(every, every, p_ssem.at[step], p_rsem.at[step], a, partner)

    starts = jnp.logical_and(a == 0, a < nx - 1)
    passes = jnp.logical_and(a > 0, a < nx - 1)

    def sent_later(step):
        if step == 0:
            if nx > 1:
                pl.when(a > 0)(rate_copy().wait_send)
            coarse_near(0).wait_send()
            for dy in range(1, ny):
                coarse_far(dy).wait_send()
                coarse_near(dy).wait_send()
            for link in links:
                when(link[0], edge_copy(link).wait_send)
                when(link[0], face_copy(0, link).wait_send)
        if step + 1 < STEPS:
            for link in links:
                when(link[0], face_copy(step + 1, link).wait_send)
                if link[4] is None:
                    when(link[0], chain_copy(step, link).wait_send)
            if nx > 1:
                pl.when(a > 0)(all_u(step).wait_send)
        all_q(step).wait_send()
        pl.when(a < nx - 1)(all_p(step).wait_send)

    for step in range(STEPS):
        last = step + 1 == STEPS
        if step == 0:
            arrives(functools.partial(face_copy, step), links[-1])
            inner = pl.ds(pl.multiple_of(in_slot * face, face), face)
            ghost = split(frecv[step, inner, :])

            def start_fill(i, carry, ghost=ghost, inner=inner):
                at = rows_of(i, block)
                back = perm_t[at, inner]
                jump[at, :] = r_buf[at, :] - dot(back, ghost[0]) - dot(back, ghost[1])
                return carry

            lax.fori_loop(0, blocks, start_fill, 0)
            for link in links[:-1]:
                arrives(functools.partial(face_copy, step), link)

            @apart
            def _(step=step):
                base[...] -= stacked3(npp[...], split(frecv[step]))

            prim = base[...]
        else:
            for link in links:
                arrives(functools.partial(face_copy, step), link)

            @apart
            def _(step=step):
                base[...] -= stacked3(npp[...], split(frecv[step]))

            for link in links:
                if link[4] is None:
                    arrives(functools.partial(chain_copy, step - 1), link)
            beside = jnp.concatenate([tall3(hrecv[step - 1, slot]) for slot in range(slots)])
            prim = base[...] + dot(couple[...], beside)
        for q in range(ng):
            psend[step, q] = pack(prim[:, q * part : (q + 1) * part])
        for dz, d in order:
            spread(step, dz, d).start()
        gath[step, me] = psend[step, g]
        if step == 0:
            outer = pl.ds(pl.multiple_of(out_slot * face, face), face)
            sides = [(pl.ds(slot * face, face)) for slot in range(xs)] + [outer]
            ghosts = [split(frecv[step, side, :]) for side in sides]
        else:
            for slot in range(slots):
                at = slice(slot * face, (slot + 1) * face)
                fix[at, :] = frecv[step, at, :] - 0.5 * dot(
                    edges[at, :], beside[slot * 3 * prims : (slot + 1) * 3 * prims]
                )
            sides = [pl.ds(0, slots * face)]
            ghosts = [split(fix[...])]

        def fill(i, carry, step=step, sides=sides, ghosts=ghosts):
            at = rows_of(i, block)
            value = jump[at, :] if step == 0 else t2_ref[at, :]
            for side, ghost in zip(sides, ghosts):
                back = perm_t[at, side]
                value = value - dot(back, ghost[0]) - dot(back, ghost[1])
            jump[at, :] = value
            high_v[at, :], low_v[at, :] = split(value)
            return carry

        lax.fori_loop(0, blocks, fill, 0)

        def multiply(i, carry):
            at = rows_of(i, block)
            work = dot3((nh[at, :], nl[at, :]), (high_v[...], low_v[...]))
            high_w[at, :], low_w[at, :] = split(work)
            return carry

        lax.fori_loop(0, blocks, multiply, 0)
        if step == 0:
            for dy in range(1, ny):
                coarse_arrived(along[dy] * 2 + core)
                coarse_near(dy).start()

        def smooth(i, carry, step=step, last=last):
            at = rows_of(i, block)
            update = dot3((dh[at, :], dl[at, :]), (high_w[...], low_w[...]))
            if step == 0:
                t1_ref[at, :] = update
            else:
                t1_ref[at, :] += update
            rest = jump[at, :] - 0.5 * update
            t2_ref[at, :] = rest
            if not last:
                high_v[at, :], low_v[at, :] = split(rest)
            return carry

        lax.fori_loop(0, blocks, smooth, 0)
        if not last:
            rests = (high_v[...], low_v[...])
            for link in links[:-1]:
                take_faces(step + 1, rests, [link])
                send_part(step + 1, 0, [link])
            take_faces(step + 1, rests, links[-1:])
            face_copy(step + 1, links[-1]).start()
        if step == 0:
            for dy in range(ny):
                coarse_arrived(along[dy] * 2 + 1 - core)
            size = ng * prims
            cs[0:size, :], cs[size : 2 * size, :] = split(
                c_all[...].reshape(size, c_all.shape[2])
            )
        if step > 0:
            sent_later(step - 1)
        all_spread(step).wait_recv()

        @apart
        def _(step=step):
            values = jnp.concatenate([unpack(gath[step, b]) for b in range(ny_all)], axis=0)
            size = ng * prims
            terms = dot(cs[...], jnp.concatenate(split(values), axis=1))
            quarter = terms[:size, :part] + terms[size:, :part] + terms[:size, part:]
            for q in range(ng):
                qsend[step, q] = pack(quarter[q * prims : (q + 1) * prims, :])

        @pl.when(starts)
        def _(step=step):
            for d in [*range(1, ng), 0]:
                first_copy(step, d).start()

        for d in range(1, ng):
            q_copy(step, d).start()
        if nx > 1 and not last:

            @pl.when(a > 0)
            def _(step=step):
                for d in [*range(1, ng), 0]:
                    down_copy(step, d).start()

        if not last:
            send_part(step + 1, 1, links[:-1])
        cown[step, g] = qsend[step, g]
        all_spread(step).wait_send()
        all_q(step).wait_recv()

        def joined(ref, step=step):
            return jnp.concatenate([unpack(ref[step, q]) for q in range(ng)], axis=1)

        chain_out = last_ref if last else hsend.at[step]

        @pl.when(a == 0)
        def _(chain_out=chain_out):
            chain_out[...] = joined(cown)

        @pl.when(a > 0)
        def _(step=step, chain_out=chain_out):
            chain_v[...] = joined(cown)
            all_p(step).wait_recv()
            chain_out[...] = chain_v[...] + rate * joined(cprev)

        @pl.when(passes)
        def _(step=step, chain_out=chain_out):
            for q in range(ng):
                csend[step, q] = pack(chain_out[:, q * part : (q + 1) * part])
                next_copy(step, q).start()

        if not last:
            for link in links:
                if link[4] is None:
                    when(link[0], chain_copy(step, link).start)
            send_part(step + 1, 2, links[:-1])
            chain = tall3(hsend[step])

            def finish(i, carry, chain=chain):
                at = rows_of(i, block)
                more = dot(thin_ref[at, :], chain)
                t1_ref[at, :] += more
                t2_ref[at, :] -= 0.5 * more
                return carry

            lax.fori_loop(0, blocks, finish, 0)
            base[...] = stacked3(sel[...], split(t2_ref[...]))
            if nx > 1:

                @pl.when(a > 0)
                def _(step=step):
                    hrecv[step, 0] = joined(cprev)

                @pl.when(a < nx - 1)
                def _(step=step):
                    if step == 0:
                        rate_copy().wait_recv()
                    all_u(step).wait_recv()
                    above_row = rate_in[0:1, :prims]
                    rate_up = jnp.sum(jnp.where(eye, above_row, 0.0), axis=1, keepdims=True)
                    hrecv[step, xs - 1] = joined(cup) + rate_up * hsend[step]
            if step == 0:
                for link in links:
                    arrives(edge_copy, link)
                for slot in range(slots):
                    at = slice(slot * face, (slot + 1) * face)
                    high, low = split(unpack(erecv[slot], prims))
                    edges[at, :] = jnp.concatenate([high, high, low], axis=1)
                    both_ways = dot(npp[:, at], edges[at, :])
                    across = both_ways[:prims, :prims] + both_ways[:prims, 2 * prims :]
                    high, low = split(0.5 * (across + both_ways[prims:, :prims]))
                    for k, piece_of in enumerate((high, high, low)):
                        left = (3 * slot + k) * prims
                        couple[:, left : left + prims] = piece_of
    sent_later(STEPS - 1)


def closing(t1, t2, thin, chain, sol, res):
    rows = sol.shape[0]
    at = pl.ds(pl.multiple_of(pl.program_id(0) * rows, rows), rows)
    more = dot(thin[at, :], tall3(chain[...]))
    sol[...] = t1[at, :] + more
    res[...] = t2[at, :] - 0.5 * more


def local(nx, ny_all, residual_in, neumann, dirichlet, coarse, decay, face_rows, primal):
    unknowns, width = residual_in.shape[2:]
    prims = primal.shape[2]
    order = coarse.shape[2]
    nz, ny = line_sizes(ny_all)
    ng = 2 * ny
    part = width // ng
    fold = max(1, 128 // part)
    piece = (prims // fold, fold * part)
    face = unknowns // 4
    slots = x_slots(nx) + 2
    anywhere = pl.BlockSpec(memory_space=pl.ANY)
    inside = pl.BlockSpec(memory_space=pltpu.VMEM)
    square = (unknowns, unknowns)
    field = (unknowns, width)
    ghosts = (slots * face, width)
    edge = (slots, face * prims // 128, 128)
    dma = pltpu.SemaphoreType.DMA
    whole = jax.ShapeDtypeStruct(field, F32)
    outs = [(field, F32), (field, F32), ((unknowns, 3 * prims), BF16), ((prims, width), F32)]
    pieces = pl.pallas_call(
        functools.partial(kernel, nx, ny_all),
        out_shape=tuple(pltpu.VMEM(shape, kind) for shape, kind in outs),
        in_specs=[anywhere] * 7,
        out_specs=(inside,) * 4,
        scratch_shapes=[
            pltpu.VMEM(square, F32),
            pltpu.VMEM(square, F32),
        ]
        + [pltpu.VMEM(square, BF16)] * 4
        + [
            pltpu.VMEM((slots * face, unknowns), BF16),
            pltpu.VMEM((unknowns, slots * face), BF16),
        ]
        + [pltpu.VMEM(field, F32)] * 2
        + [pltpu.VMEM(field, BF16)] * 4
        + [
            pltpu.VMEM((STEPS,) + ghosts, F32),
            pltpu.VMEM((STEPS,) + ghosts, F32),
            pltpu.VMEM(ghosts, F32),
            pltpu.VMEM((ng, prims, order), F32),
            pltpu.VMEM((2 * ng * prims, order), BF16),
            pltpu.VMEM((STEPS, ng) + piece, F32),
            pltpu.VMEM((STEPS, ny_all) + piece, F32),
            pltpu.VMEM((STEPS, ng) + piece, F32),
            pltpu.VMEM((STEPS, ng) + piece, F32),
            pltpu.VMEM((STEPS, ng) + piece, F32),
            pltpu.VMEM((STEPS, ng) + piece, F32),
            pltpu.VMEM((2 * prims, unknowns), BF16),
            pltpu.VMEM((2 * prims, slots * face), BF16),
            pltpu.VMEM((prims, width), F32),
            pltpu.VMEM((1, prims), F32),
            pltpu.VMEM((1, unknowns), jnp.int32),
            pltpu.VMEM((1, prims), jnp.int32),
            pltpu.VMEM(edge, F32),
            pltpu.VMEM(edge, F32),
            pltpu.VMEM((slots * face, 3 * prims), BF16),
            pltpu.VMEM((prims, slots * 3 * prims), BF16),
            pltpu.VMEM((prims, width), F32),
            pltpu.VMEM((STEPS - 1, prims, width), F32),
            pltpu.VMEM((STEPS - 1, slots, prims, width), F32),
            pltpu.VMEM((STEPS - 1, ng) + piece, F32),
            pltpu.VMEM((8, 128), F32),
            pltpu.VMEM((8, 128), F32),
            dma((4,)),
            dma((3,)),
            dma((ny,)),
            dma((ny,)),
            dma((ng,)),
            dma((STEPS, slots)),
            dma((STEPS, slots)),
            dma((STEPS,)),
            dma((STEPS,)),
            dma((STEPS,)),
            dma((STEPS,)),
            dma((STEPS,)),
            dma((STEPS,)),
            dma((slots,)),
            dma((slots,)),
            dma((STEPS - 1, slots)),
            dma((STEPS - 1, slots)),
            dma((STEPS - 1,)),
            dma((STEPS - 1,)),
            dma((2,)),
            pltpu.SemaphoreType.REGULAR((max(1, nz - 1), 2)),
        ],
        compiler_params=pltpu.CompilerParams(
            collective_id=0, has_side_effects=True, vmem_limit_bytes=62720 * 1024
        ),
    )(
        residual_in[0, 0],
        neumann[0, 0],
        dirichlet[0, 0],
        coarse[0],
        decay[0],
        face_rows[0],
        primal[0],
    )
    rows = unknowns // 2
    tall = pl.BlockSpec((rows, width), lambda i: (i, 0))
    sol, res = pl.pallas_call(
        closing,
        grid=(unknowns // rows,),
        out_shape=(whole, whole),
        in_specs=[inside] * 4,
        out_specs=(tall, tall),
        compiler_params=pltpu.CompilerParams(vmem_limit_bytes=16000 * 1024),
    )(*pieces)
    return (sol[None, None], res[None, None])


def solution(mesh):
    return jax.shard_map(
        functools.partial(local, mesh.shape["gx"], mesh.shape["gy"]),
        mesh=mesh,
        in_specs=(
            P("gx", "gy", None, None),
            P("gx", "gy", None, None),
            P("gx", "gy", None, None),
            P("gx", "gy", None),
            P("gx", "gy", None),
            P("gx", "gy", None),
            P("gx", "gy", None),
        ),
        out_specs=(P("gx", "gy", None, None), P("gx", "gy", None, None)),
        check_vma=False,
    )
```
